256 devices in a mesh: front: 64 (over z, x, core), col: 4 (over y).
Axes of the slice: x: 4, y: 4, z: 8, core: 2. Of those that a mesh axis runs over, the one named last changes fastest.
Arguments:
- leaf_load: bfloat16 [65536, 2048], P('front', 'col'), may hold values from -6 to 6
- leaf_inverse: bfloat16 [65536, 1024], P(('front', 'col')), may hold values from -0.1875 to 0.1875
- leaf_coupling: bfloat16 [32768, 1024], P('front'), may hold values from -0.1875 to 0.1875
- leaf_rowmap: int32 [64, 512], P('front'), may hold values from 0 to 511, each once within a row
- load_first: bfloat16 [16384, 2048], P('front', 'col'), may hold values from -6 to 6
- load_second: bfloat16 [8192, 2048], P('front', 'col'), may hold values from -6 to 6
- load_third: bfloat16 [4096, 2048], P('front', 'col'), may hold values from -6 to 6
- inverse_first: bfloat16 [16384, 512], P('front'), may hold values from -0.15625 to 0.15625
- inverse_second: bfloat16 [8192, 512], P('front'), may hold values from -0.15625 to 0.15625
- inverse_third: bfloat16 [4096, 512], P('front'), may hold values from -0.15625 to 0.15625
- coupling_first: bfloat16 [512, 16384], P(None, 'front'), may hold values from -0.25 to 0.25
- coupling_second: bfloat16 [512, 8192], P(None, 'front'), may hold values from -0.25 to 0.25
- rowmap_first: int32 [32, 512], replicated, may hold values from 0 to 511, each once within a row
- rowmap_second: int32 [16, 512], replicated, may hold values from 0 to 511, each once within a row
- surface_coupling: bfloat16 [192, 1024, 1024], P('front'), may hold values from -0.125 to 0.125
- neighbor_tiles: int32 [64, 2], replicated, may hold values from 0 to 63, as said below
Outputs:
- volume_solution: bfloat16 [65536, 2048], P('front', 'col')
- surface_tiles: bfloat16 [65536, 2048], P('front', 'col')
- solution_first: bfloat16 [16384, 2048], P('front', 'col')
- solution_second: bfloat16 [8192, 2048], P('front', 'col')
- solution_third: bfloat16 [4096, 2048], P('front', 'col')
The draws below stay inside these ranges and needn't reach their ends.
Inputs may be any that keep to these rules, and one draw needn't show every extreme that they name: Each row of leaf_rowmap is a permutation of the 512 separator rows. Each row of rowmap_first is a permutation of the 512 separator rows. Each row of rowmap_second is a permutation of the 512 separator rows. `neighbor_tiles`: row f names two different tiles, neither equal to f, each within 2 of f; counting each front's own tile, every tile receives 1 to 5 contributions, and some tile receives 5.
All inputs are finite; a program needn't handle non-finite values.
Results may differ from the reference program's by a relative error of at most 0.015.
Values may be sent and summed in bfloat16 or wider, within the bound.
No kernel may reach another device: no remote copies, remote signals or barrier semaphores. Data moves between devices by JAX's collectives and lax.ppermute only.
A program may use at most 128 MiB of HBM per device.

```python
import jax
import jax.numpy as jnp
from jax import lax

F = 1024
S = 512
TR = 1024
PANEL = 2048
N_FRONT = 64


def draw_neighbor_tiles(key, part):
    center_key, score_key = jax.random.split(jax.random.fold_in(key, 11))
    offsets = jnp.array([-2, -1, 1, 2], jnp.int32)
    fronts = jnp.arange(N_FRONT, dtype=jnp.int32)
    target = fronts[:, None] + offsets[None, :]
    center = jax.random.randint(center_key, (), 2, N_FRONT - 2).astype(jnp.int32)
    scores = jax.random.randint(score_key, (N_FRONT, 4), 0, 1000).astype(jnp.int32) * 4 + jnp.arange(4, dtype=jnp.int32)[None, :]
    scores = jnp.where((target < 0) | (target >= N_FRONT), scores + 100000, scores)
    scores = jnp.where(target == center, scores - 100000, scores)
    ranking = jnp.argsort(scores, axis=1)[:, :2]
    return jnp.take_along_axis(target, ranking, axis=1).astype(jnp.int32)


def block_levels(key, shape, cuts, low, top_value):
    def one(position, blocks):
        heights = jax.random.uniform(jax.random.fold_in(jax.random.fold_in(key, 6), position), (blocks,), jnp.float32, low / len(cuts), top_value / len(cuts))
        return jnp.repeat(jnp.exp(heights), shape[position] // blocks).reshape((-1,) + (1,) * (len(shape) - position - 1))

    gain = one(*cuts[0])
    for cut in cuts[1:]:
        gain = gain * one(*cut)
    return gain


def normal_values(key, dims, scale, reach, cuts=(), held_as=jnp.bfloat16):
    entries = scale * jax.random.normal(key, dims, jnp.float32)
    if cuts:
        entries = entries * block_levels(key, dims, cuts, -0.22, 0.18)
    return jnp.clip(entries, -reach, reach).astype(held_as)


def setup_inputs(seed: int = 0) -> dict:
    streams_of = jax.random.split(jax.random.key(seed), 17)
    return {
        "leaf_load": normal_values(streams_of[0], (N_FRONT * F, PANEL), 1.0, 6.0, ((0, 64), (1, 4))),
        "leaf_inverse": normal_values(streams_of[1], (N_FRONT * F, F), F ** -0.5, 0.1875, ((0, 256),)),
        "leaf_coupling": normal_values(streams_of[2], (N_FRONT * S, F), F ** -0.5, 0.1875, ((0, 64),)),
        "leaf_rowmap": jax.vmap(lambda own: jax.random.permutation(own, S))(jax.random.split(streams_of[3], N_FRONT)).reshape((N_FRONT, S)).astype(jnp.int32),
        "load_first": normal_values(streams_of[4], (N_FRONT // 2 * S, PANEL), 1.0, 6.0, ((0, 64), (1, 4))),
        "load_second": normal_values(streams_of[5], (N_FRONT // 4 * S, PANEL), 1.0, 6.0, ((0, 64), (1, 4))),
        "load_third": normal_values(streams_of[6], (N_FRONT // 8 * S, PANEL), 1.0, 6.0, ((0, 64), (1, 4))),
        "inverse_first": normal_values(streams_of[7], (N_FRONT // 2 * S, S), (3 * S) ** -0.5, 0.15625, ((0, 64),)),
        "inverse_second": normal_values(streams_of[8], (N_FRONT // 4 * S, S), (3 * S) ** -0.5, 0.15625, ((0, 64),)),
        "inverse_third": normal_values(streams_of[9], (N_FRONT // 8 * S, S), (3 * S) ** -0.5, 0.15625, ((0, 64),)),
        "coupling_first": normal_values(streams_of[10], (S, N_FRONT // 2 * S), S ** -0.5, 0.25, ((1, 64),)),
        "coupling_second": normal_values(streams_of[11], (S, N_FRONT // 4 * S), S ** -0.5, 0.25, ((1, 64),)),
        "rowmap_first": jax.vmap(lambda own: jax.random.permutation(own, S))(jax.random.split(streams_of[12], (N_FRONT // 2))).reshape((N_FRONT // 2, S)).astype(jnp.int32),
        "rowmap_second": jax.vmap(lambda own: jax.random.permutation(own, S))(jax.random.split(streams_of[13], (N_FRONT // 4))).reshape((N_FRONT // 4, S)).astype(jnp.int32),
        "surface_coupling": normal_values(streams_of[14], (N_FRONT * 3, TR, F), (2 * F) ** -0.5, 0.125, ((0, 64),)),
        "neighbor_tiles": draw_neighbor_tiles(jax.random.fold_in(streams_of[16], 71), 0),
    }


def products(left, right):
    return lax.map(lambda operands: jnp.dot(operands[0], operands[1], preferred_element_type=jnp.float32), (left, right))


def transposed(left, right):
    return lax.map(lambda operands: jnp.dot(operands[0].T, operands[1], preferred_element_type=jnp.float32), (left, right))


def gathered(values, rowmap):
    return jax.vmap(lambda current, row_index: current[row_index])(values, rowmap)


def scattered(values, rowmap):
    return jax.vmap(lambda current, row_index: jnp.zeros_like(current).at[row_index].set(current))(values, rowmap)


def slot_products(operands):
    surface, volume = operands
    return jnp.stack([jnp.dot(surface[slot], volume, preferred_element_type=jnp.float32) for slot in range(3)])


def reference(leaf_load, leaf_inverse, leaf_coupling, leaf_rowmap, load_first, load_second, load_third, inverse_first, inverse_second, inverse_third, coupling_first, coupling_second, rowmap_first, rowmap_second, surface_coupling, neighbor_tiles):
    fronts = leaf_load.shape[0] // F
    panel_cols = leaf_load.shape[1]
    leaf_right = leaf_load.reshape(fronts, F, panel_cols)
    leaf_factor = leaf_inverse.reshape(fronts, F, F)
    leaf_links = leaf_coupling.reshape(fronts, S, F)
    leaf_start = products(leaf_factor, leaf_right).astype(jnp.bfloat16)
    partial_value = gathered(products(leaf_links, leaf_start), leaf_rowmap)
    load_list = (load_first, load_second, load_third)
    inverses = (inverse_first, inverse_second, inverse_third)
    couplings = (coupling_first, coupling_second)
    rowmaps = (rowmap_first, rowmap_second)
    solved = []
    node_count = fronts
    for level_index in range(3):
        node_count = node_count // 2
        load_rows = load_list[level_index].reshape(node_count, S, panel_cols).astype(jnp.float32)
        right_side = (load_rows - partial_value[0::2] - partial_value[1::2]).astype(jnp.bfloat16)
        inverse = inverses[level_index].reshape(node_count, S, S)
        solution = products(inverse, right_side).astype(jnp.bfloat16)
        solved.append(solution)
        if level_index < 2:
            coupling = couplings[level_index].reshape(S, node_count, S).transpose(1, 0, 2)
            partial_value = gathered(products(coupling, solution), rowmaps[level_index])
    parent_rows = solved[2]
    results = [None, None, parent_rows]
    for level_index in (1, 0):
        node_count = solved[level_index].shape[0]
        lifted = scattered(jnp.repeat(parent_rows, 2, axis=0), rowmaps[level_index])
        coupling = couplings[level_index].reshape(S, node_count, S).transpose(1, 0, 2)
        pulled = transposed(coupling, lifted).astype(jnp.bfloat16)
        inverse = inverses[level_index].reshape(node_count, S, S)
        parent_rows = (solved[level_index].astype(jnp.float32) - products(inverse, pulled)).astype(jnp.bfloat16)
        results[level_index] = parent_rows
    lifted = scattered(jnp.repeat(parent_rows, 2, axis=0), leaf_rowmap)
    pulled = transposed(leaf_links, lifted).astype(jnp.bfloat16)
    volume = (leaf_start.astype(jnp.float32) - products(leaf_factor, pulled)).astype(jnp.bfloat16)
    surface = surface_coupling.reshape(fronts, 3, TR, F)
    contribution = lax.map(slot_products, (surface, volume)).astype(jnp.bfloat16)
    own_tiles = jnp.arange(fronts, dtype=jnp.int32)[:, None]
    destination = jnp.concatenate([own_tiles, neighbor_tiles.astype(jnp.int32)], axis=1).reshape(-1)
    tile_sums = jnp.zeros((fronts, TR, panel_cols), jnp.float32).at[destination].add(contribution.reshape(fronts * 3, TR, panel_cols).astype(jnp.float32))
    return (volume.reshape(fronts * F, panel_cols), tile_sums.astype(jnp.bfloat16).reshape(fronts * TR, panel_cols), results[0].reshape(-1, panel_cols), results[1].reshape(-1, panel_cols), results[2].reshape(-1, panel_cols))
```

```python
import jax
import jax.numpy as jnp
from jax import lax
from jax.sharding import PartitionSpec as P

F32 = jnp.float32
BF16 = jnp.bfloat16


def flip(x, mask):
    count = lax.axis_size("front")
    return lax.ppermute(x, "front", [(i, i ^ mask) for i in range(count)])


def shift(x, axis, steps):
    count = lax.axis_size(axis)
    return lax.ppermute(x, axis, [(i, (i + steps) % count) for i in range(count)])


def mm(a, b):
    return jnp.dot(a, b, preferred_element_type=F32)


def mm_t(a, b):
    return lax.dot_general(a, b, (((0,), (0,)), ((), ())), preferred_element_type=F32)


def in_order(pieces, place):
    return jnp.concatenate(
        [lax.select_n(place ^ i, *pieces) if len(pieces) > 2 else jnp.where(place == i, pieces[0], pieces[1]) for i in range(len(pieces))],
        axis=0,
    )


def selector(row_map):
    order = row_map.shape[0]
    return (row_map[:, None] == lax.broadcasted_iota(jnp.int32, (order, order), 1)).astype(BF16)


def embed(rows, block, count):
    hit = lax.broadcasted_iota(jnp.int32, (count, 1, 1), 0) == block
    return jnp.where(hit, rows.astype(F32)[None], 0.0).reshape(count * rows.shape[0], rows.shape[1])


def local(
    leaf_load,
    leaf_inverse,
    leaf_coupling,
    leaf_rowmap,
    load_first,
    load_second,
    load_third,
    inverse_first,
    inverse_second,
    inverse_third,
    coupling_first,
    coupling_second,
    rowmap_first,
    rowmap_second,
    surface_coupling,
    neighbor_tiles,
):
    front = lax.axis_index("front")
    col = lax.axis_index("col")
    core = front & 1
    half = leaf_load.shape[1] // 2

    def my_half(x):
        return lax.dynamic_slice_in_dim(x, core * half, half, 1)

    rows = leaf_inverse.shape[0]
    top, low = leaf_inverse[: rows // 2], leaf_inverse[rows // 2 :]
    up_top = shift(top, "col", 1)
    down_low = shift(low, "col", -1)
    up_low = shift(low, "col", 1)
    down_top = shift(top, "col", -1)
    far_top = shift(up_top, "col", 1)
    far_low = shift(down_low, "col", -1)
    behind = jnp.concatenate([up_top, up_low], axis=0)
    ahead = jnp.concatenate([down_top, down_low], axis=0)
    far = jnp.concatenate([far_top, far_low], axis=0)

    select_leaf = selector(leaf_rowmap[0])
    select_first = selector(lax.dynamic_index_in_dim(rowmap_first, front >> 1, 0, keepdims=False))
    select_second = selector(lax.dynamic_index_in_dim(rowmap_second, front >> 2, 0, keepdims=False))
    leaf_c = mm(select_leaf, leaf_coupling).astype(BF16)
    own_first = lax.dot_general(coupling_first, select_first, (((0,), (1,)), ((), ())), preferred_element_type=F32).astype(BF16)
    own_second = lax.dot_general(coupling_second, select_second, (((0,), (1,)), ((), ())), preferred_element_type=F32).astype(BF16)
    first_ct = in_order([own_first, flip(own_first, 1)], core)
    first_inv = in_order([inverse_first, flip(inverse_first, 1)], core)
    pack = jnp.concatenate([inverse_second, own_second, inverse_third, load_third], axis=0)
    pack1 = flip(pack, 1)
    pack2 = flip(pack, 2)
    pack3 = flip(pack2, 1)
    packs = [pack, pack1, pack2, pack3]
    n2, n3 = inverse_second.shape[0], inverse_third.shape[0]
    second_inv = in_order([p[:n2] for p in packs], front & 3)
    second_ct = in_order([p[n2 : 2 * n2] for p in packs], front & 3)
    third_near = in_order([p[2 * n2 : 2 * n2 + n3] for p in packs], front & 3)
    third_far = flip(third_near[: 2 * n3], 6), flip(third_near[2 * n3 :], 6)
    third_far = jnp.concatenate(third_far, axis=0)
    third_inv = in_order([third_near, third_far], (front >> 2) & 1)
    load3 = my_half(in_order([p[2 * n2 + n3 :] for p in packs], front & 3))
    load2 = my_half(in_order([load_second, flip(load_second, 1)], core))

    blocks = [mm(x, leaf_load).astype(BF16) for x in (leaf_inverse, ahead, far, behind)]
    rotated = jnp.concatenate(blocks, axis=0)
    leaf_start = jnp.concatenate(
        [lax.select_n((i - col) & 3, *blocks) for i in range(4)], axis=0
    )
    factor = jnp.concatenate(
        [lax.select_n((i - col) & 3, leaf_inverse, ahead, far, behind) for i in range(4)], axis=0
    )

    term = embed(load_first, core, 2) - mm(leaf_c, leaf_start)
    mine = my_half(term)
    other = lax.dynamic_slice_in_dim(term, (1 - core) * half, half, 1).astype(BF16)
    rhs = (mine + flip(other, 1).astype(F32)).astype(BF16)
    y_first = mm(first_inv, rhs).astype(BF16)
    term = embed(load2, (front >> 1) & 1, 2) - mm_t(first_ct, y_first)
    rhs = (term + flip(term.astype(BF16), 2).astype(F32)).astype(BF16)
    y_second = mm(second_inv, rhs).astype(BF16)
    term = embed(load3, (front >> 2) & 1, 2) - mm_t(second_ct, y_second)
    rhs = (term + flip(term.astype(BF16), 6).astype(F32)).astype(BF16)
    sol_third = mm(third_inv, rhs).astype(BF16)

    pull = mm(second_ct, sol_third).astype(BF16)
    sol_second = (y_second.astype(F32) - mm(second_inv, pull)).astype(BF16)
    pull = mm(first_ct, sol_second).astype(BF16)
    sol_first = (y_first.astype(F32) - mm(first_inv, pull)).astype(BF16)

    def both_halves(own, partner):
        return jnp.where(
            core == 0,
            jnp.concatenate([own, partner], axis=1),
            jnp.concatenate([partner, own], axis=1),
        )

    def my_rows(solution, count, place):
        own = lax.dynamic_slice_in_dim(solution, place * count, count, 0)
        away = lax.dynamic_slice_in_dim(solution, (place ^ 1) * count, count, 0)
        return both_halves(own, flip(away, 1))

    first_full = both_halves(sol_first, flip(sol_first, 1))
    out_first = lax.dynamic_slice_in_dim(first_full, core * load_first.shape[0], load_first.shape[0], 0)
    out_second = my_rows(sol_second, n2, front & 3)
    out_third = my_rows(sol_third, n3, front & 7)

    pulled = mm_t(leaf_c, first_full).astype(BF16)
    volume = (leaf_start.astype(F32) - mm(factor, pulled)).astype(BF16)
    aimed = lax.dynamic_index_in_dim(neighbor_tiles, front, 0, keepdims=False)
    c_own = mm(surface_coupling[0], volume)
    c_one = mm(surface_coupling[1], volume).astype(BF16)
    c_two = mm(surface_coupling[2], volume).astype(BF16)

    def aimed_at(offset):
        tile = front + offset
        return jnp.where(aimed[0] == tile, c_one, jnp.where(aimed[1] == tile, c_two, jnp.zeros_like(c_one)))

    inner = jnp.where(core == 0, 1, -1)
    near = flip(aimed_at(inner), 1)
    relay = flip(aimed_at(-inner), 1)
    forward = aimed_at(2)
    forward = jnp.where(core == 0, forward + relay, forward)
    backward = aimed_at(-2)
    backward = jnp.where(core == 1, backward + relay, backward)
    from_back = shift(forward, "front", 2)
    from_ahead = shift(backward, "front", -2)
    tiles = c_own + near.astype(F32) + from_back.astype(F32) + from_ahead.astype(F32)
    return (volume, tiles.astype(BF16), out_first, out_second, out_third)


def solution(mesh):
    return jax.shard_map(
        local,
        mesh=mesh,
        in_specs=(
            P("front", "col"),
            P(("front", "col"), None),
            P("front", None),
            P("front", None),
            P("front", "col"),
            P("front", "col"),
            P("front", "col"),
            P("front", None),
            P("front", None),
            P("front", None),
            P(None, "front"),
            P(None, "front"),
            P(),
            P(),
            P("front", None, None),
            P(),
        ),
        out_specs=(P("front", "col"),) * 5,
        check_vma=False,
    )
```

```python
import functools

import jax
import jax.numpy as jnp
from jax import lax
from jax.experimental import pallas as pl
from jax.experimental.pallas import tpu as pltpu
from jax.sharding import PartitionSpec as P

F32 = jnp.float32
BF16 = jnp.bfloat16


def flip(x, mask):
    count = lax.axis_size("front")
    return lax.ppermute(x, "front", [(i, i ^ mask) for i in range(count)])


def shift(x, axis, steps):
    count = lax.axis_size(axis)
    return lax.ppermute(x, axis, [(i, (i + steps) % count) for i in range(count)])


def pass_on(x, axis, steps):
    count = lax.axis_size(axis)
    return lax.ppermute(x, axis, [(i, i + steps) for i in range(count) if 0 <= i + steps < count])


def mm(a, b):
    return jnp.dot(a, b, preferred_element_type=F32)


def mm_t(a, b):
    return lax.dot_general(a, b, (((0,), (0,)), ((), ())), preferred_element_type=F32)


class Held:
    def __init__(self, source, target, sem):
        self.copy = pltpu.make_async_copy(source, target, sem)
        self.target = target
        self.shape = target.shape
        self.copy.start()

    def wait(self):
        self.copy.wait()

    def __getitem__(self, index):
        return self.target[index]


def kernel(body, outs, args, flops=1e9, fetched=(), scalars=(), scratch=()):
    vmem = pl.BlockSpec(memory_space=pltpu.VMEM)
    specs = [pl.BlockSpec(memory_space=pltpu.HBM) if i in fetched else vmem for i in range(len(args))]
    nbytes = sum(a.size * a.dtype.itemsize for a in args)
    order = sorted(fetched)
    shapes = [cut_shape(fetched, i, args[i]) for i in order]

    def run(*refs):
        ins, rest = list(refs[: len(args)]), refs[len(args) :]
        numbers, rest = rest[: len(scalars)], rest[len(scalars) :]
        results, rest = rest[: len(outs)], rest[len(outs) :]
        own, rest = rest[: len(scratch)], rest[len(scratch) :]
        for k, i in enumerate(order):
            source = ins[i]
            if isinstance(fetched, dict) and fetched[i]:
                source = source.at[fetched[i]]
            ins[i] = Held(source, rest[k], rest[len(order)].at[k])
        body(*ins, *numbers, *results, *own)

    extra = [pltpu.VMEM(shape, args[i].dtype) for i, shape in zip(order, shapes)]
    if order:
        extra.append(pltpu.SemaphoreType.DMA((len(order),)))
    args = [pltpu.with_memory_space_constraint(a, pltpu.HBM) if i in fetched else a for i, a in enumerate(args)]
    return pl.pallas_call(
        run,
        out_shape=[jax.ShapeDtypeStruct(s, t) for s, t in outs],
        in_specs=specs + [pl.BlockSpec(memory_space=pltpu.SMEM)] * len(scalars),
        out_specs=[vmem] * len(outs),
        scratch_shapes=list(scratch) + extra,
        compiler_params=pltpu.CompilerParams(vmem_limit_bytes=10 << 20),
        cost_estimate=pl.CostEstimate(flops=int(flops), bytes_accessed=nbytes, transcendentals=0),
    )(*args, *scalars)


def cut_shape(fetched, i, array):
    cut = fetched[i] if isinstance(fetched, dict) else None
    if not cut:
        return array.shape
    return tuple(len(range(*c.indices(n))) for c, n in zip(cut, array.shape, strict=True))


def block(i, size):
    return pl.ds(pl.multiple_of(i * size, size), size)


def each(count, size, step):
    lax.fori_loop(0, count // size, lambda i, carry: (step(block(i, size)), carry)[1], 0)


def selector_t(row_map):
    order = row_map.shape[1]
    return (row_map == lax.broadcasted_iota(jnp.int32, (order, order), 0)).astype(BF16)


def pack_body(rm1, rm2, d_own, e_own, inv1, inv2, inv3, load2, load3, aimed, out_x, out_c, out_aim):
    front = lax.axis_index("front")
    n2, n3 = inv2.shape[0], inv3.shape[0]
    for x in (rm1, rm2, d_own, e_own, inv1, inv2, inv3, load2, load3):
        x.wait()
    select = selector_t(rm2[pl.ds(front >> 2, 1), :])
    e_t = mm_t(e_own[...], select).astype(BF16)
    out_x[:n2, :] = inv2[...]
    out_x[n2 : 2 * n2, :] = e_t
    out_x[2 * n2 : 2 * n2 + n3, :] = inv3[...]
    out_x[2 * n2 + n3 :, :] = load3[...]
    select = selector_t(rm1[pl.ds(front >> 1, 1), :])
    n1 = inv1.shape[0]
    out_c[:n1, :] = mm_t(d_own[...], select).astype(BF16)
    out_c[n1 : 2 * n1, :] = inv1[...]
    out_c[2 * n1 :, :] = load2[...]
    row = lax.broadcasted_iota(jnp.int32, out_aim.shape, 0)
    out_aim[...] = jnp.where(row == 0, aimed[front, 0] - front, aimed[front, 1] - front)


def leaf_weight_body(rm, c, out_c, out_ct):
    select = selector_t(rm[...])
    size = 256

    def step(i, carry):
        cols = block(i, size)
        own = c[:, cols]
        out_c[:, cols] = mm_t(select, own).astype(BF16)
        out_ct[cols, :] = mm_t(own, select).astype(BF16)
        return carry

    lax.fori_loop(0, c.shape[1] // size, step, 0)


def leaf_term(pieces, columns, c, size):
    col = lax.axis_index("col")
    total = 0.0
    for piece, place in pieces:
        cols = pl.ds(pl.multiple_of(((2 * col + place) & 7) * size, size), piece.shape[0])
        total = total + mm(c[:, cols], mm(piece[...], columns).astype(BF16))
    return total


def near_body(own, up_top, down_low, b, c, load1, out_other, out_mine):
    core = lax.axis_index("front") & 1
    half, size = b.shape[1] // 2, up_top.shape[0]
    for out, which in ((out_other, 1 - core), (out_mine, core)):
        out[...] = -leaf_term(((own, 0), (up_top, 6), (down_low, 3)), b[:, block(which, half)], c, size)
        rows = block(core, load1.shape[0])
        out[rows, :] += load1[:, block(which, half)].astype(F32)


def far_term(up_low, down_top, far_top, far_low, b, c, near, which):
    half, size = b.shape[1] // 2, far_top.shape[0]
    pieces = ((up_low, 7), (down_top, 2), (far_top, 4), (far_low, 5))
    return near[...] - leaf_term(pieces, b[:, block(which, half)], c, size)


def other_body(up_low, down_top, far_top, far_low, b, c, near, out):
    core = lax.axis_index("front") & 1
    out[...] = far_term(up_low, down_top, far_top, far_low, b, c, near, 1 - core).astype(BF16)


def mine_body(up_low, down_top, far_top, far_low, b, c, near, out):
    core = lax.axis_index("front") & 1
    out[...] = far_term(up_low, down_top, far_top, far_low, b, c, near, core)


def first_weight_body(pack, away, load_half, out_d, out_dt, out_inv, out_load):
    front = lax.axis_index("front")
    core = front & 1
    n1 = out_inv.shape[0] // 2
    n2 = away.shape[0] - 2 * n1
    half = out_load.shape[1]
    out_load[...] = jnp.zeros_like(out_load)
    for piece, place in ((pack, core), (away, 1 - core)):
        rows = block(place, n1)
        t = piece[:n1, :]
        out_dt[rows, :] = t
        out_d[:, rows] = t.T
        out_inv[rows, :] = piece[n1 : 2 * n1, :]
        where = block(2 * ((front >> 1) & 1) + place, n2)
        out_load[where, :] = piece[2 * n1 :, block(core, half)]


def second_weight_body(p0, p1, p2, p3, out_e, out_et, out_inv, out_load, out_third):
    front = lax.axis_index("front")
    core = front & 1
    n2 = out_inv.shape[0] // 4
    n3 = n2 // 2
    half = out_load.shape[1]
    out_load[...] = jnp.zeros_like(out_load)
    for mask, piece in enumerate((p0, p1, p2, p3)):
        place = (front & 3) ^ mask
        rows = block(place, n2)
        t = piece[n2 : 2 * n2, :]
        out_inv[rows, :] = piece[:n2, :]
        out_et[rows, :] = t
        out_e[:, rows] = t.T
        out_third[block(place, n3), :] = piece[2 * n2 : 2 * n2 + n3, :]
        out_load[block(((front >> 2) & 1) * 4 + place, n3), :] = piece[2 * n2 + n3 :, block(core, half)]


def first_body(mine, other, inv, d, load2, out_rhs, out_term):
    rhs = (mine[...].astype(F32) + other[...].astype(F32)).astype(BF16)
    out_rhs[...] = rhs
    y = mm(inv[...], rhs).astype(BF16)
    out_term[...] = (load2[...].astype(F32) - mm(d[...], y)).astype(BF16)


def second_body(mine, other, inv, e, load3, out_rhs, out_term):
    first_body(mine, other, inv, e, load3, out_rhs, out_term)


def down_body(mine, other, third_near, third_far, e_t, inv2, rhs2, d_t, inv1, rhs1, out1, own2, away2, own3, away3, out3, out2):
    front = lax.axis_index("front")
    bit = (front >> 2) & 1
    rhs = (mine[...].astype(F32) + other[...].astype(F32)).astype(BF16)
    rows = third_near.shape[0]
    out3[block(bit, rows), :] = mm(third_near[...], rhs).astype(BF16)
    out3[block(1 - bit, rows), :] = mm(third_far[...], rhs).astype(BF16)
    left = (rhs2[...].astype(F32) - mm(e_t[...], out3[...])).astype(BF16)
    sol = mm(inv2[...], left).astype(BF16)
    out2[...] = sol
    left = (rhs1[...].astype(F32) - mm(d_t[...], sol)).astype(BF16)
    out1[...] = mm(inv1[...], left).astype(BF16)
    for own, away, whole, place in ((own2, away2, out2, front & 3), (own3, away3, out3, front & 7)):
        own[...] = whole[block(place, own.shape[0]), :]
        away[...] = whole[block(place ^ 1, own.shape[0]), :]


def stage_body(c_t, b, surface, own, up_top, up_low, down_top, down_low, far_top, far_low, out_ct, out_b, out_surface, out_factor, sems):
    col = lax.axis_index("col")
    size = up_top.shape[0]
    pairs = [(c_t, out_ct), (b, out_b)]
    for piece, place in ((own, 0), (up_top, 6), (up_low, 7), (down_top, 2), (down_low, 3), (far_top, 4), (far_low, 5)):
        rows = pl.ds(pl.multiple_of(((2 * col + place) & 7) * size, size), piece.shape[0])
        pairs.append((piece, out_factor.at[rows, :]))
    pairs.append((surface, out_surface))
    copies = [pltpu.make_async_copy(x, y, sems.at[i]) for i, (x, y) in enumerate(pairs)]
    for copy in copies:
        copy.start()
    for copy in copies:
        copy.wait()


def volume_body(part, c_t, b, factor, surface, s_own, s_away, aim, *rest):
    out, out_v, out_near, out_relay, out_up, out_down, left, sem = rest[-8:]
    front = lax.axis_index("front")
    core = front & 1
    half = out_v.shape[1]
    side = jnp.where(core == part, s_own[...], s_away[...])

    def start(rows):
        left[rows, :] = (b[rows, part * half : (part + 1) * half].astype(F32) - mm(c_t[rows, :], side)).astype(BF16)

    def solve(rows):
        out_v[rows, :] = mm(factor[rows, :], left[...]).astype(BF16)

    each(b.shape[0], 256, start)
    each(b.shape[0], 256, solve)
    store = pltpu.make_async_copy(out_v, out.at[:, part * half : (part + 1) * half], sem)
    store.start()
    inner = 1 - 2 * core

    def tiles(rows):
        v = out_v[...]
        c_one = mm(surface[1, rows, :], v).astype(BF16)
        c_two = mm(surface[2, rows, :], v).astype(BF16)
        zero = jnp.zeros_like(c_one)
        one = jnp.broadcast_to(aim[0:1, 0:1], c_one.shape)
        two = jnp.broadcast_to(aim[1:2, 0:1], c_one.shape)
        for out, offset in ((out_near, inner), (out_relay, -inner), (out_up, 2), (out_down, -2)):
            out[rows, :] = jnp.where(one == offset, c_one, jnp.where(two == offset, c_two, zero))

    each(surface.shape[1], 256, tiles)
    store.wait()


def sum_body(up, down, relay, out_up, out_down):
    core = lax.axis_index("front") & 1

    @pl.when(core == 0)
    def _():
        out_up[...] = up[...] + relay[...]
        out_down[...] = down[...]

    @pl.when(core == 1)
    def _():
        out_up[...] = up[...]
        out_down[...] = down[...] + relay[...]


def outs_body(first, first_away, second, second_away, third, third_away, out1, out2, out3, t1, t2, t3, sems):
    core = lax.axis_index("front") & 1
    half = first.shape[1]
    rows = block(core, t1.shape[0])
    copies = []
    for i, (own, away, out, total) in enumerate(((first.at[rows, :], first_away.at[rows, :], out1, t1), (second, second_away, out2, t2), (third, third_away, out3, t3))):
        total[:, block(core, half)] = own[...]
        total[:, block(1 - core, half)] = away[...]
        copies.append(pltpu.make_async_copy(total, out, sems.at[i]))
        copies[-1].start()
    for copy in copies:
        copy.wait()


def own_body(surface, v, out):
    def tiles(rows):
        out[rows, :] = mm(surface[0, rows, :], v[...]).astype(BF16)

    each(surface.shape[1], 256, tiles)


def finish_body(part, own, near, back, ahead, *rest):
    out, total, sem = rest[-3:]
    half = own.shape[1]

    def tiles(rows):
        total[rows, :] = (
            own[rows, :].astype(F32) + near[rows, :].astype(F32) + back[rows, :].astype(F32) + ahead[rows, :].astype(F32)
        ).astype(BF16)

    each(own.shape[0], 256, tiles)
    store = pltpu.make_async_copy(total, out.at[:, part * half : (part + 1) * half], sem)
    store.start()
    store.wait()


VMEM = pl.BlockSpec(memory_space=pltpu.VMEM)
SMEM = pl.BlockSpec(memory_space=pltpu.SMEM)
HBM = pl.BlockSpec(memory_space=pltpu.HBM)


def halves(body, args, scalars, extra_outs, scratch, whole, flops):
    shape = jax.ShapeDtypeStruct((args[0].shape[0], 2 * extra_outs[0].shape[1]), BF16) if whole is None else whole
    more = () if whole is None else (whole,)
    return pl.pallas_call(
        body,
        out_shape=[jax.ShapeDtypeStruct(shape.shape, BF16)] + extra_outs[1:],
        in_specs=[VMEM] * len(args) + [SMEM] * len(scalars) + [HBM] * len(more),
        out_specs=[HBM] + [VMEM] * len(extra_outs[1:]),
        scratch_shapes=scratch + [pltpu.SemaphoreType.DMA],
        input_output_aliases={len(args) + len(scalars): 0} if more else {},
        compiler_params=pltpu.CompilerParams(vmem_limit_bytes=12 << 20),
        cost_estimate=pl.CostEstimate(flops=int(flops), bytes_accessed=8 << 20, transcendentals=0),
    )(*args, *scalars, *more)


def stage(args):
    shapes = [args[0].shape, args[1].shape, args[2].shape, (args[0].shape[0],) * 2]
    args = [pltpu.with_memory_space_constraint(a, pltpu.HBM) for a in args]
    return pl.pallas_call(
        stage_body,
        out_shape=[jax.ShapeDtypeStruct(x, BF16) for x in shapes],
        in_specs=[HBM] * len(args),
        out_specs=[VMEM] * 4,
        scratch_shapes=[pltpu.SemaphoreType.DMA((len(args),))],
        compiler_params=pltpu.CompilerParams(vmem_limit_bytes=12 << 20),
        cost_estimate=pl.CostEstimate(flops=0, bytes_accessed=10 << 20, transcendentals=0),
        name="stage",
    )(*args)


def local(
    leaf_load,
    leaf_inverse,
    leaf_coupling,
    leaf_rowmap,
    load_first,
    load_second,
    load_third,
    inverse_first,
    inverse_second,
    inverse_third,
    coupling_first,
    coupling_second,
    rowmap_first,
    rowmap_second,
    surface_coupling,
    neighbor_tiles,
):
    full, panel = leaf_load.shape
    half = panel // 2
    order = leaf_coupling.shape[0]
    square = ((order, order), BF16)
    column = ((order, half), BF16)

    rows = leaf_inverse.shape[0]
    top, low = leaf_inverse[: rows // 2], leaf_inverse[rows // 2 :]
    up_top = shift(top, "col", 1)
    down_low = shift(low, "col", -1)
    up_low = shift(low, "col", 1)
    down_top = shift(top, "col", -1)
    far_top = shift(up_top, "col", 1)
    far_low = shift(down_low, "col", -1)

    n1, n2, n3 = inverse_first.shape[0], inverse_second.shape[0], inverse_third.shape[0]
    pack_x, pack_c, aim = kernel(
        pack_body,
        [((2 * n2 + 2 * n3, order), BF16), ((2 * n1 + n2, order), BF16), ((8, 128), jnp.int32)],
        (rowmap_first, rowmap_second, coupling_first, coupling_second, inverse_first, inverse_second, inverse_third, load_second, load_third),
        fetched=range(9),
        scalars=(neighbor_tiles,),
    )
    pack2 = flip(pack_x, 2)
    pack1 = flip(pack_x, 1)
    away_c = flip(pack_c, 1)
    leaf_c, leaf_ct = kernel(
        leaf_weight_body, [((order, full), BF16), ((full, order), BF16)], (leaf_rowmap, leaf_coupling)
    )
    first_d, first_dt, first_inv, load2 = kernel(
        first_weight_body, [square, square, square, column], (pack_c, away_c, load_second)
    )
    pack3 = flip(pack2, 1)
    second_e, second_et, second_inv, load3, third_near = kernel(
        second_weight_body, [square, square, square, column, ((order // 2, order), BF16)], (pack_x, pack1, pack2, pack3)
    )
    third_far = flip(third_near, 6)

    near_other, near_mine = kernel(
        near_body, [((order, half), F32)] * 2, (leaf_inverse, up_top, down_low, leaf_load, leaf_c, load_first), 2e9
    )
    (other,) = kernel(other_body, [column], (up_low, down_top, far_top, far_low, leaf_load, leaf_c, near_other))
    other = flip(other, 1)
    (mine,) = kernel(mine_body, [((order, half), F32)], (up_low, down_top, far_top, far_low, leaf_load, leaf_c, near_mine))
    rhs_first, term = kernel(first_body, [column] * 2, (mine, other, first_inv, first_d, load2))
    away = flip(term, 2)
    rhs_second, term = kernel(second_body, [column] * 2, (term, away, second_inv, second_e, load3))
    away = flip(term, 6)
    staged = stage((leaf_ct, leaf_load, surface_coupling, leaf_inverse, up_top, up_low, down_top, down_low, far_top, far_low))
    sol_first, second_own, second_away, third_own, third_away = kernel(
        down_body,
        [column, ((n2, half), BF16), ((n2, half), BF16), ((n3, half), BF16), ((n3, half), BF16)],
        (term, away, third_near, third_far, second_et, second_inv, rhs_second, first_dt, first_inv, rhs_first),
        scratch=[pltpu.VMEM(*column)] * 2,
    )
    sol_away = flip(sol_first, 1)

    tail = []
    out_volume = out_tiles = None
    part_shape = jax.ShapeDtypeStruct((full, half), BF16)
    part_scratch = pltpu.VMEM((full, half), BF16)
    for part in range(2):
        out_volume, volume, near, relay, ahead_sum, back_sum = halves(
            functools.partial(volume_body, part),
            (staged[0], staged[1], staged[3], staged[2], sol_first, sol_away, aim),
            (),
            [part_shape] * 6,
            [part_scratch],
            out_volume,
            3e9,
        )
        relay = flip(relay, 1)
        ahead_sum, back_sum = kernel(sum_body, [((full, half), BF16)] * 2, (ahead_sum, back_sum, relay), 1e6)
        from_back = pass_on(ahead_sum, "front", 2)
        from_ahead = pass_on(back_sum, "front", -2)
        near = flip(near, 1)
        (c_own,) = kernel(own_body, [((full, half), BF16)], (staged[2], volume))
        tail.append((c_own, near, from_back, from_ahead))
    for part, terms in enumerate(tail):
        (out_tiles,) = halves(
            functools.partial(finish_body, part), terms, (), [part_shape], [part_scratch], out_tiles, 1e6
        )

    second_away = flip(second_away, 1)
    third_away = flip(third_away, 1)
    shapes = [(n1, panel), (n2, panel), (n3, panel)]
    out_first, out_second, out_third = pl.pallas_call(
        outs_body,
        out_shape=[jax.ShapeDtypeStruct(x, BF16) for x in shapes],
        in_specs=[VMEM] * 6,
        out_specs=[HBM] * 3,
        scratch_shapes=[pltpu.VMEM(x, BF16) for x in shapes] + [pltpu.SemaphoreType.DMA((3,))],
        compiler_params=pltpu.CompilerParams(vmem_limit_bytes=4 << 20),
        cost_estimate=pl.CostEstimate(flops=0, bytes_accessed=1 << 20, transcendentals=0),
        name="outs",
    )(sol_first, sol_away, second_own, second_away, third_own, third_away)
    return (out_volume, out_tiles, out_first, out_second, out_third)


def solution(mesh):
    return jax.shard_map(
        local,
        mesh=mesh,
        in_specs=(
            P("front", "col"),
            P(("front", "col"), None),
            P("front", None),
            P("front", None),
            P("front", "col"),
            P("front", "col"),
            P("front", "col"),
            P("front", None),
            P("front", None),
            P("front", None),
            P(None, "front"),
            P(None, "front"),
            P(),
            P(),
            P("front", None, None),
            P(),
        ),
        out_specs=(P("front", "col"),) * 5,
        check_vma=False,
    )
```

```python
import functools

import jax
import jax.numpy as jnp
from jax import lax
from jax.experimental import pallas as pl
from jax.experimental.pallas import tpu as pltpu
from jax.sharding import PartitionSpec as P

F32 = jnp.float32
BF16 = jnp.bfloat16


def flip(x, mask):
    count = lax.axis_size("front")
    return lax.ppermute(x, "front", [(i, i ^ mask) for i in range(count)])


def shift(x, axis, steps):
    count = lax.axis_size(axis)
    return lax.ppermute(x, axis, [(i, (i + steps) % count) for i in range(count)])


def swap_next(x):
    count = lax.axis_size("front")
    pairs = [(i, i + 2 if i >> 1 & 1 else i - 2) for i in range(count)]
    return lax.ppermute(x, "front", [(i, j) for i, j in pairs if 0 <= j < count])


def mm(a, b):
    return jnp.dot(a, b, preferred_element_type=F32)


def mm_t(a, b):
    return lax.dot_general(a, b, (((0,), (0,)), ((), ())), preferred_element_type=F32)


class Held:
    def __init__(self, source, target, sem):
        self.copy = pltpu.make_async_copy(source, target, sem)
        self.target = target
        self.shape = target.shape
        self.copy.start()

    def wait(self):
        self.copy.wait()

    def __getitem__(self, index):
        return self.target[index]


def kernel(body, outs, args, flops=1e9, fetched=(), scalars=(), scratch=()):
    vmem = pl.BlockSpec(memory_space=pltpu.VMEM)
    specs = [pl.BlockSpec(memory_space=pltpu.HBM) if i in fetched else vmem for i in range(len(args))]
    nbytes = sum(a.size * a.dtype.itemsize for a in args)
    order = sorted(fetched)
    shapes = [cut_shape(fetched, i, args[i]) for i in order]

    def run(*refs):
        ins, rest = list(refs[: len(args)]), refs[len(args) :]
        numbers, rest = rest[: len(scalars)], rest[len(scalars) :]
        results, rest = rest[: len(outs)], rest[len(outs) :]
        own, rest = rest[: len(scratch)], rest[len(scratch) :]
        for k, i in enumerate(order):
            source = ins[i]
            if isinstance(fetched, dict) and fetched[i]:
                source = source.at[fetched[i]]
            ins[i] = Held(source, rest[k], rest[len(order)].at[k])
        body(*ins, *numbers, *results, *own)

    extra = [pltpu.VMEM(shape, args[i].dtype) for i, shape in zip(order, shapes)]
    if order:
        extra.append(pltpu.SemaphoreType.DMA((len(order),)))
    args = [pltpu.with_memory_space_constraint(a, pltpu.HBM) if i in fetched else a for i, a in enumerate(args)]
    return pl.pallas_call(
        run,
        out_shape=[jax.ShapeDtypeStruct(s, t) for s, t in outs],
        in_specs=specs + [pl.BlockSpec(memory_space=pltpu.SMEM)] * len(scalars),
        out_specs=[vmem] * len(outs),
        scratch_shapes=list(scratch) + extra,
        compiler_params=pltpu.CompilerParams(vmem_limit_bytes=10 << 20),
        cost_estimate=pl.CostEstimate(flops=int(flops), bytes_accessed=nbytes, transcendentals=0),
    )(*args, *scalars)


def cut_shape(fetched, i, array):
    cut = fetched[i] if isinstance(fetched, dict) else None
    if not cut:
        return array.shape
    return tuple(len(range(*c.indices(n))) for c, n in zip(cut, array.shape, strict=True))


def block(i, size):
    return pl.ds(pl.multiple_of(i * size, size), size)


def each(count, size, step):
    lax.fori_loop(0, count // size, lambda i, carry: (step(block(i, size)), carry)[1], 0)


def selector_t(row_map):
    order = row_map.shape[1]
    return (row_map == lax.broadcasted_iota(jnp.int32, (order, order), 0)).astype(BF16)


def pack_body(rm1, rm2, d_own, e_own, inv1, inv2, inv3, load2, load3, aimed, out_x, out_c, out_aim):
    front = lax.axis_index("front")
    n2, n3 = inv2.shape[0], inv3.shape[0]
    for x in (rm1, rm2, d_own, e_own, inv1, inv2, inv3, load2, load3):
        x.wait()
    select = selector_t(rm2[pl.ds(front >> 2, 1), :])
    e_t = mm_t(e_own[...], select).astype(BF16)
    out_x[:n2, :] = inv2[...]
    out_x[n2 : 2 * n2, :] = e_t
    out_x[2 * n2 : 2 * n2 + n3, :] = inv3[...]
    out_x[2 * n2 + n3 :, :] = load3[...]
    select = selector_t(rm1[pl.ds(front >> 1, 1), :])
    n1 = inv1.shape[0]
    out_c[:n1, :] = mm_t(d_own[...], select).astype(BF16)
    out_c[n1 : 2 * n1, :] = inv1[...]
    out_c[2 * n1 :, :] = load2[...]
    row = lax.broadcasted_iota(jnp.int32, out_aim.shape, 0)
    out_aim[...] = jnp.where(row == 0, aimed[front, 0] - front, aimed[front, 1] - front)


def leaf_weight_body(rm, c, out_c, out_ct):
    select = selector_t(rm[...])
    size = 256

    def step(i, carry):
        cols = block(i, size)
        own = c[:, cols]
        out_c[:, cols] = mm_t(select, own).astype(BF16)
        out_ct[cols, :] = mm_t(own, select).astype(BF16)
        return carry

    lax.fori_loop(0, c.shape[1] // size, step, 0)


def leaf_term(pieces, columns, c, size):
    col = lax.axis_index("col")
    total = 0.0
    for piece, place in pieces:
        cols = pl.ds(pl.multiple_of(((2 * col + place) & 7) * size, size), piece.shape[0])
        total = total + mm(c[:, cols], mm(piece[...], columns).astype(BF16))
    return total


def near_body(own, up_top, down_low, b, c, load1, out_other, out_mine):
    core = lax.axis_index("front") & 1
    half, size = b.shape[1] // 2, up_top.shape[0]
    for out, which in ((out_other, 1 - core), (out_mine, core)):
        out[...] = -leaf_term(((own, 0), (up_top, 6), (down_low, 3)), b[:, block(which, half)], c, size)
        rows = block(core, load1.shape[0])
        out[rows, :] += load1[:, block(which, half)].astype(F32)


def far_term(up_low, down_top, far_top, far_low, b, c, near, which):
    half, size = b.shape[1] // 2, far_top.shape[0]
    pieces = ((up_low, 7), (down_top, 2), (far_top, 4), (far_low, 5))
    return near[...] - leaf_term(pieces, b[:, block(which, half)], c, size)


def other_body(up_low, down_top, far_top, far_low, b, c, near, out):
    core = lax.axis_index("front") & 1
    out[...] = far_term(up_low, down_top, far_top, far_low, b, c, near, 1 - core).astype(BF16)


def mine_body(up_low, down_top, far_top, far_low, b, c, near, out):
    core = lax.axis_index("front") & 1
    out[...] = far_term(up_low, down_top, far_top, far_low, b, c, near, core)


def first_weight_body(pack, away, load_half, out_d, out_dt, out_inv, out_load):
    front = lax.axis_index("front")
    core = front & 1
    n1 = out_inv.shape[0] // 2
    n2 = away.shape[0] - 2 * n1
    half = out_load.shape[1]
    out_load[...] = jnp.zeros_like(out_load)
    for piece, place in ((pack, core), (away, 1 - core)):
        rows = block(place, n1)
        t = piece[:n1, :]
        out_dt[rows, :] = t
        out_d[:, rows] = t.T
        out_inv[rows, :] = piece[n1 : 2 * n1, :]
        where = block(2 * ((front >> 1) & 1) + place, n2)
        out_load[where, :] = piece[2 * n1 :, block(core, half)]


def second_weight_body(p0, p1, p2, p3, out_e, out_et, out_inv, out_load, out_third):
    front = lax.axis_index("front")
    core = front & 1
    n2 = out_inv.shape[0] // 4
    n3 = n2 // 2
    half = out_load.shape[1]
    out_load[...] = jnp.zeros_like(out_load)
    for mask, piece in enumerate((p0, p1, p2, p3)):
        place = (front & 3) ^ mask
        rows = block(place, n2)
        t = piece[n2 : 2 * n2, :]
        out_inv[rows, :] = piece[:n2, :]
        out_et[rows, :] = t
        out_e[:, rows] = t.T
        out_third[block(place, n3), :] = piece[2 * n2 : 2 * n2 + n3, :]
        out_load[block(((front >> 2) & 1) * 4 + place, n3), :] = piece[2 * n2 + n3 :, block(core, half)]


def first_body(mine, other, inv, d, load2, out_rhs, out_term):
    rhs = (mine[...].astype(F32) + other[...].astype(F32)).astype(BF16)
    out_rhs[...] = rhs
    y = mm(inv[...], rhs).astype(BF16)
    out_term[...] = (load2[...].astype(F32) - mm(d[...], y)).astype(BF16)


def second_body(mine, other, inv, e, load3, out_rhs, out_term):
    first_body(mine, other, inv, e, load3, out_rhs, out_term)


def down_body(mine, other, third_near, third_far, e_t, inv2, rhs2, d_t, inv1, rhs1, out1, own2, away2, own3, away3, out3, out2):
    front = lax.axis_index("front")
    bit = (front >> 2) & 1
    rhs = (mine[...].astype(F32) + other[...].astype(F32)).astype(BF16)
    rows = third_near.shape[0]
    out3[block(bit, rows), :] = mm(third_near[...], rhs).astype(BF16)
    out3[block(1 - bit, rows), :] = mm(third_far[...], rhs).astype(BF16)
    left = (rhs2[...].astype(F32) - mm(e_t[...], out3[...])).astype(BF16)
    sol = mm(inv2[...], left).astype(BF16)
    out2[...] = sol
    left = (rhs1[...].astype(F32) - mm(d_t[...], sol)).astype(BF16)
    out1[...] = mm(inv1[...], left).astype(BF16)
    for own, away, whole, place in ((own2, away2, out2, front & 3), (own3, away3, out3, front & 7)):
        own[...] = whole[block(place, own.shape[0]), :]
        away[...] = whole[block(place ^ 1, own.shape[0]), :]


def stage_body(c_t, b, surface, own, up_top, up_low, down_top, down_low, far_top, far_low, out_ct, out_b, out_surface, out_factor, sems):
    col = lax.axis_index("col")
    size = up_top.shape[0]
    pairs = [(c_t, out_ct), (b, out_b)]
    for piece, place in ((own, 0), (up_top, 6), (up_low, 7), (down_top, 2), (down_low, 3), (far_top, 4), (far_low, 5)):
        rows = pl.ds(pl.multiple_of(((2 * col + place) & 7) * size, size), piece.shape[0])
        pairs.append((piece, out_factor.at[rows, :]))
    pairs.append((surface, out_surface))
    copies = [pltpu.make_async_copy(x, y, sems.at[i]) for i, (x, y) in enumerate(pairs)]
    for copy in copies:
        copy.start()
    for copy in copies:
        copy.wait()


def volume_body(part, c_t, b, factor, surface, s_own, s_away, aim, *rest):
    out, out_v, out_near, out_relay, out_up, out_down, left, sem = rest[-8:]
    front = lax.axis_index("front")
    core = front & 1
    half = out_v.shape[1]
    side = jnp.where(core == part, s_own[...], s_away[...])

    def start(rows):
        left[rows, :] = (b[rows, part * half : (part + 1) * half].astype(F32) - mm(c_t[rows, :], side)).astype(BF16)

    def solve(rows):
        out_v[rows, :] = mm(factor[rows, :], left[...]).astype(BF16)

    each(b.shape[0], 256, start)
    each(b.shape[0], 256, solve)
    store = pltpu.make_async_copy(out_v, out.at[:, part * half : (part + 1) * half], sem)
    store.start()
    inner = 1 - 2 * core

    def tiles(rows):
        v = out_v[...]
        c_one = mm(surface[1, rows, :], v).astype(BF16)
        c_two = mm(surface[2, rows, :], v).astype(BF16)
        zero = jnp.zeros_like(c_one)
        one = jnp.broadcast_to(aim[0:1, 0:1], c_one.shape)
        two = jnp.broadcast_to(aim[1:2, 0:1], c_one.shape)
        for out, offset in ((out_near, inner), (out_relay, -inner), (out_up, 2), (out_down, -2)):
            out[rows, :] = jnp.where(one == offset, c_one, jnp.where(two == offset, c_two, zero))

    each(surface.shape[1], 256, tiles)
    store.wait()


def sum_body(up, down, relay, out_inner, out_outer):
    front = lax.axis_index("front")
    core = front & 1
    even = (front >> 1) & 1 == 0
    for which in (0, 1):
        for parity in (True, False):

            @pl.when((core == which) & (even == parity))
            def _():
                to_up, to_down = (out_inner, out_outer) if parity else (out_outer, out_inner)
                to_up[...] = up[...] + relay[...] if which == 0 else up[...]
                to_down[...] = down[...] + relay[...] if which == 1 else down[...]


def outs_body(first, first_away, second, second_away, third, third_away, out1, out2, out3, t1, t2, t3, sems):
    core = lax.axis_index("front") & 1
    half = first.shape[1]
    rows = block(core, t1.shape[0])
    copies = []
    for i, (own, away, out, total) in enumerate(((first.at[rows, :], first_away.at[rows, :], out1, t1), (second, second_away, out2, t2), (third, third_away, out3, t3))):
        total[:, block(core, half)] = own[...]
        total[:, block(1 - core, half)] = away[...]
        copies.append(pltpu.make_async_copy(total, out, sems.at[i]))
        copies[-1].start()
    for copy in copies:
        copy.wait()


def own_body(surface, v, out):
    def tiles(rows):
        out[rows, :] = mm(surface[0, rows, :], v[...]).astype(BF16)

    each(surface.shape[1], 256, tiles)


def finish_body(part, own, near, back, ahead, *rest):
    out, total, sem = rest[-3:]
    half = own.shape[1]

    def tiles(rows):
        total[rows, :] = (
            own[rows, :].astype(F32) + near[rows, :].astype(F32) + back[rows, :].astype(F32) + ahead[rows, :].astype(F32)
        ).astype(BF16)

    each(own.shape[0], 256, tiles)
    store = pltpu.make_async_copy(total, out.at[:, part * half : (part + 1) * half], sem)
    store.start()
    store.wait()


VMEM = pl.BlockSpec(memory_space=pltpu.VMEM)
SMEM = pl.BlockSpec(memory_space=pltpu.SMEM)
HBM = pl.BlockSpec(memory_space=pltpu.HBM)


def halves(body, args, scalars, extra_outs, scratch, whole, flops):
    shape = jax.ShapeDtypeStruct((args[0].shape[0], 2 * extra_outs[0].shape[1]), BF16) if whole is None else whole
    more = () if whole is None else (whole,)
    return pl.pallas_call(
        body,
        out_shape=[jax.ShapeDtypeStruct(shape.shape, BF16)] + extra_outs[1:],
        in_specs=[VMEM] * len(args) + [SMEM] * len(scalars) + [HBM] * len(more),
        out_specs=[HBM] + [VMEM] * len(extra_outs[1:]),
        scratch_shapes=scratch + [pltpu.SemaphoreType.DMA],
        input_output_aliases={len(args) + len(scalars): 0} if more else {},
        compiler_params=pltpu.CompilerParams(vmem_limit_bytes=12 << 20),
        cost_estimate=pl.CostEstimate(flops=int(flops), bytes_accessed=8 << 20, transcendentals=0),
    )(*args, *scalars, *more)


def stage(args):
    shapes = [args[0].shape, args[1].shape, args[2].shape, (args[0].shape[0],) * 2]
    args = [pltpu.with_memory_space_constraint(a, pltpu.HBM) for a in args]
    return pl.pallas_call(
        stage_body,
        out_shape=[jax.ShapeDtypeStruct(x, BF16) for x in shapes],
        in_specs=[HBM] * len(args),
        out_specs=[VMEM] * 4,
        scratch_shapes=[pltpu.SemaphoreType.DMA((len(args),))],
        compiler_params=pltpu.CompilerParams(vmem_limit_bytes=12 << 20),
        cost_estimate=pl.CostEstimate(flops=0, bytes_accessed=10 << 20, transcendentals=0),
        name="stage",
    )(*args)


def local(
    leaf_load,
    leaf_inverse,
    leaf_coupling,
    leaf_rowmap,
    load_first,
    load_second,
    load_third,
    inverse_first,
    inverse_second,
    inverse_third,
    coupling_first,
    coupling_second,
    rowmap_first,
    rowmap_second,
    surface_coupling,
    neighbor_tiles,
):
    full, panel = leaf_load.shape
    half = panel // 2
    order = leaf_coupling.shape[0]
    square = ((order, order), BF16)
    column = ((order, half), BF16)

    rows = leaf_inverse.shape[0]
    top, low = leaf_inverse[: rows // 2], leaf_inverse[rows // 2 :]
    up_top = shift(top, "col", 1)
    down_low = shift(low, "col", -1)
    up_low = shift(low, "col", 1)
    down_top = shift(top, "col", -1)
    far_top = shift(up_top, "col", 1)
    far_low = shift(down_low, "col", -1)

    n1, n2, n3 = inverse_first.shape[0], inverse_second.shape[0], inverse_third.shape[0]
    pack_x, pack_c, aim = kernel(
        pack_body,
        [((2 * n2 + 2 * n3, order), BF16), ((2 * n1 + n2, order), BF16), ((8, 128), jnp.int32)],
        (rowmap_first, rowmap_second, coupling_first, coupling_second, inverse_first, inverse_second, inverse_third, load_second, load_third),
        fetched=range(9),
        scalars=(neighbor_tiles,),
    )
    pack2 = flip(pack_x, 2)
    pack1 = flip(pack_x, 1)
    away_c = flip(pack_c, 1)
    leaf_c, leaf_ct = kernel(
        leaf_weight_body, [((order, full), BF16), ((full, order), BF16)], (leaf_rowmap, leaf_coupling)
    )
    first_d, first_dt, first_inv, load2 = kernel(
        first_weight_body, [square, square, square, column], (pack_c, away_c, load_second)
    )
    pack3 = flip(pack2, 1)
    second_e, second_et, second_inv, load3, third_near = kernel(
        second_weight_body, [square, square, square, column, ((order // 2, order), BF16)], (pack_x, pack1, pack2, pack3)
    )
    third_far = flip(third_near, 6)

    near_other, near_mine = kernel(
        near_body, [((order, half), F32)] * 2, (leaf_inverse, up_top, down_low, leaf_load, leaf_c, load_first), 2e9
    )
    (other,) = kernel(other_body, [column], (up_low, down_top, far_top, far_low, leaf_load, leaf_c, near_other))
    other = flip(other, 1)
    (mine,) = kernel(mine_body, [((order, half), F32)], (up_low, down_top, far_top, far_low, leaf_load, leaf_c, near_mine))
    rhs_first, term = kernel(first_body, [column] * 2, (mine, other, first_inv, first_d, load2))
    away = flip(term, 2)
    rhs_second, term = kernel(second_body, [column] * 2, (term, away, second_inv, second_e, load3))
    away = flip(term, 6)
    staged = stage((leaf_ct, leaf_load, surface_coupling, leaf_inverse, up_top, up_low, down_top, down_low, far_top, far_low))
    sol_first, second_own, second_away, third_own, third_away = kernel(
        down_body,
        [column, ((n2, half), BF16), ((n2, half), BF16), ((n3, half), BF16), ((n3, half), BF16)],
        (term, away, third_near, third_far, second_et, second_inv, rhs_second, first_dt, first_inv, rhs_first),
        scratch=[pltpu.VMEM(*column)] * 2,
    )
    sol_away = flip(sol_first, 1)

    tail = []
    out_volume = out_tiles = None
    part_shape = jax.ShapeDtypeStruct((full, half), BF16)
    part_scratch = pltpu.VMEM((full, half), BF16)
    for part in range(2):
        out_volume, volume, near, relay, ahead_sum, back_sum = halves(
            functools.partial(volume_body, part),
            (staged[0], staged[1], staged[3], staged[2], sol_first, sol_away, aim),
            (),
            [part_shape] * 6,
            [part_scratch],
            out_volume,
            3e9,
        )
        relay = flip(relay, 1)
        inner, outer = kernel(sum_body, [((full, half), BF16)] * 2, (ahead_sum, back_sum, relay), 1e6)
        from_outer = swap_next(outer)
        from_inner = flip(inner, 2)
        near = flip(near, 1)
        (c_own,) = kernel(own_body, [((full, half), BF16)], (staged[2], volume))
        tail.append((c_own, near, from_outer, from_inner))
    for part, terms in enumerate(tail):
        (out_tiles,) = halves(
            functools.partial(finish_body, part), terms, (), [part_shape], [part_scratch], out_tiles, 1e6
        )

    second_away = flip(second_away, 1)
    third_away = flip(third_away, 1)
    shapes = [(n1, panel), (n2, panel), (n3, panel)]
    out_first, out_second, out_third = pl.pallas_call(
        outs_body,
        out_shape=[jax.ShapeDtypeStruct(x, BF16) for x in shapes],
        in_specs=[VMEM] * 6,
        out_specs=[HBM] * 3,
        scratch_shapes=[pltpu.VMEM(x, BF16) for x in shapes] + [pltpu.SemaphoreType.DMA((3,))],
        compiler_params=pltpu.CompilerParams(vmem_limit_bytes=4 << 20),
        cost_estimate=pl.CostEstimate(flops=0, bytes_accessed=1 << 20, transcendentals=0),
        name="outs",
    )(sol_first, sol_away, second_own, second_away, third_own, third_away)
    return (out_volume, out_tiles, out_first, out_second, out_third)


def solution(mesh):
    return jax.shard_map(
        local,
        mesh=mesh,
        in_specs=(
            P("front", "col"),
            P(("front", "col"), None),
            P("front", None),
            P("front", None),
            P("front", "col"),
            P("front", "col"),
            P("front", "col"),
            P("front", None),
            P("front", None),
            P("front", None),
            P(None, "front"),
            P(None, "front"),
            P(),
            P(),
            P("front", None, None),
            P(),
        ),
        out_specs=(P("front", "col"),) * 5,
        check_vma=False,
    )
```

```python
import functools

import jax
import jax.numpy as jnp
from jax import lax
from jax.experimental import pallas as pl
from jax.experimental.pallas import tpu as pltpu
from jax.sharding import PartitionSpec as P

F32 = jnp.float32
BF16 = jnp.bfloat16


def flip(x, mask):
    count = lax.axis_size("front")
    return lax.ppermute(x, "front", [(i, i ^ mask) for i in range(count)])


def shift(x, axis, steps):
    count = lax.axis_size(axis)
    return lax.ppermute(x, axis, [(i, (i + steps) % count) for i in range(count)])


def swap_next(x):
    count = lax.axis_size("front")
    pairs = [(i, i + 2 if i >> 1 & 1 else i - 2) for i in range(count)]
    return lax.ppermute(x, "front", [(i, j) for i, j in pairs if 0 <= j < count])


def mm(a, b):
    return jnp.dot(a, b, preferred_element_type=F32)


def mm_t(a, b):
    return lax.dot_general(a, b, (((0,), (0,)), ((), ())), preferred_element_type=F32)


class Held:
    def __init__(self, source, target, sem):
        self.copy = pltpu.make_async_copy(source, target, sem)
        self.target = target
        self.shape = target.shape
        self.copy.start()

    def wait(self):
        self.copy.wait()

    def __getitem__(self, index):
        return self.target[index]


def kernel(body, outs, args, flops=1e9, fetched=(), scalars=(), scratch=()):
    vmem = pl.BlockSpec(memory_space=pltpu.VMEM)
    specs = [pl.BlockSpec(memory_space=pltpu.HBM) if i in fetched else vmem for i in range(len(args))]
    nbytes = sum(a.size * a.dtype.itemsize for a in args)
    order = sorted(fetched)
    shapes = [cut_shape(fetched, i, args[i]) for i in order]

    def run(*refs):
        ins, rest = list(refs[: len(args)]), refs[len(args) :]
        numbers, rest = rest[: len(scalars)], rest[len(scalars) :]
        results, rest = rest[: len(outs)], rest[len(outs) :]
        own, rest = rest[: len(scratch)], rest[len(scratch) :]
        for k, i in enumerate(order):
            source = ins[i]
            if isinstance(fetched, dict) and fetched[i]:
                source = source.at[fetched[i]]
            ins[i] = Held(source, rest[k], rest[len(order)].at[k])
        body(*ins, *numbers, *results, *own)

    extra = [pltpu.VMEM(shape, args[i].dtype) for i, shape in zip(order, shapes)]
    if order:
        extra.append(pltpu.SemaphoreType.DMA((len(order),)))
    args = [pltpu.with_memory_space_constraint(a, pltpu.HBM) if i in fetched else a for i, a in enumerate(args)]
    return pl.pallas_call(
        run,
        out_shape=[jax.ShapeDtypeStruct(s, t) for s, t in outs],
        in_specs=specs + [pl.BlockSpec(memory_space=pltpu.SMEM)] * len(scalars),
        out_specs=[vmem] * len(outs),
        scratch_shapes=list(scratch) + extra,
        compiler_params=pltpu.CompilerParams(vmem_limit_bytes=10 << 20),
        cost_estimate=pl.CostEstimate(flops=int(flops), bytes_accessed=nbytes, transcendentals=0),
    )(*args, *scalars)


def cut_shape(fetched, i, array):
    cut = fetched[i] if isinstance(fetched, dict) else None
    if not cut:
        return array.shape
    return tuple(len(range(*c.indices(n))) for c, n in zip(cut, array.shape, strict=True))


def block(i, size):
    return pl.ds(pl.multiple_of(i * size, size), size)


def each(count, size, step):
    lax.fori_loop(0, count // size, lambda i, carry: (step(block(i, size)), carry)[1], 0)


def selector_t(row_map):
    order = row_map.shape[1]
    return (row_map == lax.broadcasted_iota(jnp.int32, (order, order), 0)).astype(BF16)


def pack_body(rm1, rm2, d_own, e_own, inv1, inv2, inv3, load2, load3, aimed, out_x, out_c, out_aim):
    front = lax.axis_index("front")
    n2, n3 = inv2.shape[0], inv3.shape[0]
    for x in (rm1, rm2, d_own, e_own, inv1, inv2, inv3, load2, load3):
        x.wait()
    select = selector_t(rm2[pl.ds(front >> 2, 1), :])
    e_t = mm_t(e_own[...], select).astype(BF16)
    out_x[:n2, :] = inv2[...]
    out_x[n2 : 2 * n2, :] = e_t
    out_x[2 * n2 : 2 * n2 + n3, :] = inv3[...]
    out_x[2 * n2 + n3 :, :] = load3[...]
    select = selector_t(rm1[pl.ds(front >> 1, 1), :])
    n1 = inv1.shape[0]
    out_c[:n1, :] = mm_t(d_own[...], select).astype(BF16)
    out_c[n1 : 2 * n1, :] = inv1[...]
    out_c[2 * n1 :, :] = load2[...]
    row = lax.broadcasted_iota(jnp.int32, out_aim.shape, 0)
    out_aim[...] = jnp.where(row == 0, aimed[front, 0] - front, aimed[front, 1] - front)


def leaf_weight_body(rm, c, out_c, out_ct):
    rm.wait()
    c.wait()
    select = selector_t(rm[...])
    size = 256

    def step(i, carry):
        cols = block(i, size)
        own = c[:, cols]
        out_c[:, cols] = mm_t(select, own).astype(BF16)
        out_ct[cols, :] = mm_t(own, select).astype(BF16)
        return carry

    lax.fori_loop(0, c.shape[1] // size, step, 0)


def leaf_term(pieces, columns, c, size):
    col = lax.axis_index("col")
    total = 0.0
    for piece, place in pieces:
        cols = pl.ds(pl.multiple_of(((2 * col + place) & 7) * size, size), piece.shape[0])
        total = total + mm(c[:, cols], mm(piece[...], columns).astype(BF16))
    return total


def near_body(own, up_top, down_low, b, c, load1, out_other, out_mine):
    core = lax.axis_index("front") & 1
    half, size = b.shape[1] // 2, up_top.shape[0]
    for out, which in ((out_other, 1 - core), (out_mine, core)):
        out[...] = -leaf_term(((own, 0), (up_top, 6), (down_low, 3)), b[:, block(which, half)], c, size)
        rows = block(core, load1.shape[0])
        out[rows, :] += load1[:, block(which, half)].astype(F32)


def far_term(up_low, down_top, far_top, far_low, b, c, near, which):
    half, size = b.shape[1] // 2, far_top.shape[0]
    pieces = ((up_low, 7), (down_top, 2), (far_top, 4), (far_low, 5))
    return near[...] - leaf_term(pieces, b[:, block(which, half)], c, size)


def other_body(up_low, down_top, far_top, far_low, b, c, near, out):
    core = lax.axis_index("front") & 1
    out[...] = far_term(up_low, down_top, far_top, far_low, b, c, near, 1 - core).astype(BF16)


def mine_body(up_low, down_top, far_top, far_low, b, c, near, out):
    core = lax.axis_index("front") & 1
    out[...] = far_term(up_low, down_top, far_top, far_low, b, c, near, core)


def first_weight_body(pack, away, load_half, out_d, out_dt, out_inv, out_load):
    front = lax.axis_index("front")
    core = front & 1
    n1 = out_inv.shape[0] // 2
    n2 = away.shape[0] - 2 * n1
    half = out_load.shape[1]
    out_load[...] = jnp.zeros_like(out_load)
    for piece, place in ((pack, core), (away, 1 - core)):
        rows = block(place, n1)
        t = piece[:n1, :]
        out_dt[rows, :] = t
        out_d[:, rows] = t.T
        out_inv[rows, :] = piece[n1 : 2 * n1, :]
        where = block(2 * ((front >> 1) & 1) + place, n2)
        out_load[where, :] = piece[2 * n1 :, block(core, half)]


def second_weight_body(p0, p1, p2, p3, out_e, out_et, out_inv, out_load, out_third):
    front = lax.axis_index("front")
    core = front & 1
    n2 = out_inv.shape[0] // 4
    n3 = n2 // 2
    half = out_load.shape[1]
    out_load[...] = jnp.zeros_like(out_load)
    for mask, piece in enumerate((p0, p1, p2, p3)):
        place = (front & 3) ^ mask
        rows = block(place, n2)
        t = piece[n2 : 2 * n2, :]
        out_inv[rows, :] = piece[:n2, :]
        out_et[rows, :] = t
        out_e[:, rows] = t.T
        out_third[block(place, n3), :] = piece[2 * n2 : 2 * n2 + n3, :]
        out_load[block(((front >> 2) & 1) * 4 + place, n3), :] = piece[2 * n2 + n3 :, block(core, half)]


def first_body(mine, other, inv, d, load2, out_rhs, *terms):
    rhs = (mine[...] + other[...].astype(F32)).astype(BF16)
    out_rhs[...] = rhs
    y = mm(inv[...], rhs).astype(BF16)
    term = (load2[...].astype(F32) - mm(d[...], y)).astype(BF16)
    size = term.shape[1] // len(terms)
    for i, out in enumerate(terms):
        out[...] = term[:, i * size : (i + 1) * size]


def second_body(part, mine, other, inv, e, load3, out_rhs, out_term):
    size = mine.shape[1]
    rhs = (mine[...].astype(F32) + other[...].astype(F32)).astype(BF16)
    out_rhs[...] = rhs
    y = mm(inv[...], rhs).astype(BF16)
    out_term[...] = (load3[:, part * size : (part + 1) * size].astype(F32) - mm(e[...], y)).astype(BF16)


def down_body(part, mine, other, third_near, third_far, e_t, inv2, rhs2, d_t, inv1, rhs1, out1, own2, away2, own3, away3, out3, out2):
    front = lax.axis_index("front")
    bit = (front >> 2) & 1
    size = mine.shape[1]
    rhs = (mine[...].astype(F32) + other[...].astype(F32)).astype(BF16)
    rows = third_near.shape[0]
    out3[block(bit, rows), :] = mm(third_near[...], rhs).astype(BF16)
    out3[block(1 - bit, rows), :] = mm(third_far[...], rhs).astype(BF16)
    left = (rhs2[...].astype(F32) - mm(e_t[...], out3[...])).astype(BF16)
    sol = mm(inv2[...], left).astype(BF16)
    out2[...] = sol
    left = (rhs1[:, part * size : (part + 1) * size].astype(F32) - mm(d_t[...], sol)).astype(BF16)
    out1[...] = mm(inv1[...], left).astype(BF16)
    for own, away, whole, place in ((own2, away2, out2, front & 3), (own3, away3, out3, front & 7)):
        own[...] = whole[block(place, own.shape[0]), :]
        away[...] = whole[block(place ^ 1, own.shape[0]), :]


def merge_body(second_a, second_b, third_a, third_b, out):
    rows, size = second_a.shape
    out[:rows, :size] = second_a[...]
    out[:rows, size:] = second_b[...]
    out[rows:, :size] = third_a[...]
    out[rows:, size:] = third_b[...]


def copy_all(pairs, sems):
    copies = [pltpu.make_async_copy(x, y, sems.at[i]) for i, (x, y) in enumerate(pairs)]
    for copy in copies:
        copy.start()
    for copy in copies:
        copy.wait()


def stage_body(b, surface, out_b, out_surface, sems):
    copy_all([(b, out_b), (surface, out_surface)], sems)


def factor_body(own, up_top, up_low, down_top, down_low, far_top, far_low, out, sems):
    col = lax.axis_index("col")
    size = up_top.shape[0]
    pairs = []
    for piece, place in ((own, 0), (up_top, 6), (up_low, 7), (down_top, 2), (down_low, 3), (far_top, 4), (far_low, 5)):
        rows = pl.ds(pl.multiple_of(((2 * col + place) & 7) * size, size), piece.shape[0])
        pairs.append((piece, out.at[rows, :]))
    copy_all(pairs, sems)


def chunk_of(core, part, size):
    return slice((2 * core + part) * size, (2 * core + part + 1) * size)


def store_chunks(source, out, part, size, sems):
    stores = []
    for i in (0, 1):
        stores.append(
            pltpu.make_async_copy(source.at[:, i * size : (i + 1) * size], out.at[:, chunk_of(i, part, size)], sems.at[i])
        )
        stores[-1].start()
    return stores


def volume_body(part, c_t, b, factor, surface, s_own, s_away, aim, *rest):
    out, out_v, out_near, out_relay, out_up, out_down, left, sems = rest[-8:]
    core = lax.axis_index("front") & 1
    size = s_own.shape[1]
    sides = (jnp.where(core == 0, s_own[...], s_away[...]), jnp.where(core == 0, s_away[...], s_own[...]))
    side = jnp.concatenate(sides, axis=1)

    def start(rows):
        load = jnp.concatenate([b[rows, chunk_of(i, part, size)] for i in (0, 1)], axis=1)
        left[rows, :] = (load.astype(F32) - mm(c_t[rows, :], side)).astype(BF16)

    def solve(rows):
        out_v[rows, :] = mm(factor[rows, :], left[...]).astype(BF16)

    each(b.shape[0], 256, start)
    each(b.shape[0], 256, solve)
    stores = store_chunks(out_v, out, part, size, sems)
    inner = 1 - 2 * core

    def tiles(rows):
        v = out_v[...]
        c_one = mm(surface[1, rows, :], v).astype(BF16)
        c_two = mm(surface[2, rows, :], v).astype(BF16)
        zero = jnp.zeros_like(c_one)
        one = jnp.broadcast_to(aim[0:1, 0:1], c_one.shape)
        two = jnp.broadcast_to(aim[1:2, 0:1], c_one.shape)
        for out, offset in ((out_near, inner), (out_relay, -inner), (out_up, 2), (out_down, -2)):
            out[rows, :] = jnp.where(one == offset, c_one, jnp.where(two == offset, c_two, zero))

    each(surface.shape[1], 256, tiles)
    for store in stores:
        store.wait()


def sum_body(up, down, relay, out_inner, out_outer):
    front = lax.axis_index("front")
    core = front & 1
    even = (front >> 1) & 1 == 0
    for which in (0, 1):
        for parity in (True, False):

            @pl.when((core == which) & (even == parity))
            def _():
                to_up, to_down = (out_inner, out_outer) if parity else (out_outer, out_inner)
                to_up[...] = up[...] + relay[...] if which == 0 else up[...]
                to_down[...] = down[...] + relay[...] if which == 1 else down[...]


def outs_body(first_a, first_b, first_away_a, first_away_b, second_a, second_b, third_a, third_b, away, out1, out2, out3, t1, t2, t3, sems):
    core = lax.axis_index("front") & 1
    size = first_a.shape[1]
    rows = block(core, t1.shape[0])
    n2 = t2.shape[0]
    copies = []
    for i, (out, total, own, theirs) in enumerate((
        (out1, t1, (first_a.at[rows, :], first_b.at[rows, :]), (first_away_a.at[rows, :], first_away_b.at[rows, :])),
        (out2, t2, (second_a, second_b), (away.at[:n2, :size], away.at[:n2, size:])),
        (out3, t3, (third_a, third_b), (away.at[n2:, :size], away.at[n2:, size:])),
    )):
        for part in (0, 1):
            total[:, block(2 * core + part, size)] = own[part][...]
            total[:, block(2 * (1 - core) + part, size)] = theirs[part][...]
        copies.append(pltpu.make_async_copy(total, out, sems.at[i]))
        copies[-1].start()
    for copy in copies:
        copy.wait()


def own_body(surface, v, out):
    def tiles(rows):
        out[rows, :] = mm(surface[0, rows, :], v[...]).astype(BF16)

    each(surface.shape[1], 256, tiles)


def finish_body(part, own, near, back, ahead, *rest):
    out, total, sems = rest[-3:]

    def tiles(rows):
        total[rows, :] = (
            own[rows, :].astype(F32) + near[rows, :].astype(F32) + back[rows, :].astype(F32) + ahead[rows, :].astype(F32)
        ).astype(BF16)

    each(own.shape[0], 256, tiles)
    for store in store_chunks(total, out, part, own.shape[1] // 2, sems):
        store.wait()


VMEM = pl.BlockSpec(memory_space=pltpu.VMEM)
SMEM = pl.BlockSpec(memory_space=pltpu.SMEM)
HBM = pl.BlockSpec(memory_space=pltpu.HBM)


def halves(body, args, scalars, extra_outs, scratch, whole, flops):
    shape = jax.ShapeDtypeStruct((args[0].shape[0], 2 * extra_outs[0].shape[1]), BF16) if whole is None else whole
    more = () if whole is None else (whole,)
    return pl.pallas_call(
        body,
        out_shape=[jax.ShapeDtypeStruct(shape.shape, BF16)] + extra_outs[1:],
        in_specs=[VMEM] * len(args) + [SMEM] * len(scalars) + [HBM] * len(more),
        out_specs=[HBM] + [VMEM] * len(extra_outs[1:]),
        scratch_shapes=scratch + [pltpu.SemaphoreType.DMA((2,))],
        input_output_aliases={len(args) + len(scalars): 0} if more else {},
        compiler_params=pltpu.CompilerParams(vmem_limit_bytes=12 << 20),
        cost_estimate=pl.CostEstimate(flops=int(flops), bytes_accessed=8 << 20, transcendentals=0),
    )(*args, *scalars, *more)


def stage(body, shapes, args):
    args = [pltpu.with_memory_space_constraint(a, pltpu.HBM) for a in args]
    return pl.pallas_call(
        body,
        out_shape=[jax.ShapeDtypeStruct(x, BF16) for x in shapes],
        in_specs=[HBM] * len(args),
        out_specs=[VMEM] * len(shapes),
        scratch_shapes=[pltpu.SemaphoreType.DMA((len(args),))],
        compiler_params=pltpu.CompilerParams(vmem_limit_bytes=2 << 20),
        cost_estimate=pl.CostEstimate(flops=0, bytes_accessed=8 << 20, transcendentals=0),
    )(*args)


def local(
    leaf_load,
    leaf_inverse,
    leaf_coupling,
    leaf_rowmap,
    load_first,
    load_second,
    load_third,
    inverse_first,
    inverse_second,
    inverse_third,
    coupling_first,
    coupling_second,
    rowmap_first,
    rowmap_second,
    surface_coupling,
    neighbor_tiles,
):
    full, panel = leaf_load.shape
    half = panel // 2
    order = leaf_coupling.shape[0]
    square = ((order, order), BF16)
    column = ((order, half), BF16)

    rows = leaf_inverse.shape[0]
    top, low = leaf_inverse[: rows // 2], leaf_inverse[rows // 2 :]
    up_top = shift(top, "col", 1)
    down_low = shift(low, "col", -1)
    up_low = shift(low, "col", 1)
    down_top = shift(top, "col", -1)
    far_top = shift(up_top, "col", 1)
    far_low = shift(down_low, "col", -1)

    n1, n2, n3 = inverse_first.shape[0], inverse_second.shape[0], inverse_third.shape[0]
    pack_x, pack_c, aim = kernel(
        pack_body,
        [((2 * n2 + 2 * n3, order), BF16), ((2 * n1 + n2, order), BF16), ((8, 128), jnp.int32)],
        (rowmap_first, rowmap_second, coupling_first, coupling_second, inverse_first, inverse_second, inverse_third, load_second, load_third),
        fetched=range(9),
        scalars=(neighbor_tiles,),
    )
    pack2 = flip(pack_x, 2)
    pack1 = flip(pack_x, 1)
    away_c = flip(pack_c, 1)
    leaf_c, leaf_ct = kernel(
        leaf_weight_body, [((order, full), BF16), ((full, order), BF16)], (leaf_rowmap, leaf_coupling), fetched=range(2)
    )
    first_d, first_dt, first_inv, load2 = kernel(
        first_weight_body, [square, square, square, column], (pack_c, away_c, load_second)
    )
    pack3 = flip(pack2, 1)
    second_e, second_et, second_inv, load3, third_near = kernel(
        second_weight_body, [square, square, square, column, ((order // 2, order), BF16)], (pack_x, pack1, pack2, pack3)
    )
    third_far = flip(third_near, 6)

    near_other, near_mine = kernel(
        near_body, [((order, half), F32)] * 2, (leaf_inverse, up_top, down_low, leaf_load, leaf_c, load_first), 2e9
    )
    (other,) = kernel(other_body, [column], (up_low, down_top, far_top, far_low, leaf_load, leaf_c, near_other))
    other = flip(other, 1)
    (mine,) = kernel(mine_body, [((order, half), F32)], (up_low, down_top, far_top, far_low, leaf_load, leaf_c, near_mine))
    piece = ((order, half // 2), BF16)
    rhs_first, *terms = kernel(first_body, [column, piece, piece], (mine, other, first_inv, first_d, load2))
    aways = []
    for part in range(2):
        aways.append(flip(terms[part], 2))
    load, surface = stage(stage_body, [leaf_load.shape, surface_coupling.shape], (leaf_load, surface_coupling))
    (factor,) = stage(factor_body, [(full, full)], (leaf_inverse, up_top, up_low, down_top, down_low, far_top, far_low))
    rhs_second, aways_second, terms_second = [], [], []
    for part in range(2):
        rhs, term = kernel(
            functools.partial(second_body, part),
            [piece, piece],
            (terms[part], aways[part], second_inv, second_e, load3),
        )
        aways_second.append(flip(term, 6))
        rhs_second.append(rhs)
        terms_second.append(term)
    firsts, firsts_away, small = [], [], []
    for part in range(2):
        first, *rest = kernel(
            functools.partial(down_body, part),
            [piece] + [((n, half // 2), BF16) for n in (n2, n2, n3, n3)],
            (terms_second[part], aways_second[part], third_near, third_far, second_et, second_inv, rhs_second[part], first_dt, first_inv, rhs_first),
            scratch=[pltpu.VMEM(*piece)] * 2,
        )
        firsts_away.append(flip(first, 1))
        firsts.append(first)
        small.append(rest)

    tail = []
    out_volume = out_tiles = None
    part_shape = jax.ShapeDtypeStruct((full, half), BF16)
    part_scratch = pltpu.VMEM((full, half), BF16)
    for part in range(2):
        out_volume, volume, near, relay, ahead_sum, back_sum = halves(
            functools.partial(volume_body, part),
            (leaf_ct, load, factor, surface, firsts[part], firsts_away[part], aim),
            (),
            [part_shape] * 6,
            [part_scratch],
            out_volume,
            3e9,
        )
        relay = flip(relay, 1)
        inner, outer = kernel(sum_body, [((full, half), BF16)] * 2, (ahead_sum, back_sum, relay), 1e6)
        from_outer = swap_next(outer)
        from_inner = flip(inner, 2)
        near = flip(near, 1)
        (c_own,) = kernel(own_body, [((full, half), BF16)], (surface, volume))
        tail.append((c_own, near, from_outer, from_inner))
    for part, terms in enumerate(tail):
        (out_tiles,) = halves(
            functools.partial(finish_body, part), terms, (), [part_shape], [part_scratch], out_tiles, 1e6
        )

    (away,) = kernel(merge_body, [((n2 + n3, half), BF16)], (small[0][1], small[1][1], small[0][3], small[1][3]), 1e6)
    away = flip(away, 1)
    shapes = [(n1, panel), (n2, panel), (n3, panel)]
    out_first, out_second, out_third = pl.pallas_call(
        outs_body,
        out_shape=[jax.ShapeDtypeStruct(x, BF16) for x in shapes],
        in_specs=[VMEM] * 9,
        out_specs=[HBM] * 3,
        scratch_shapes=[pltpu.VMEM(x, BF16) for x in shapes] + [pltpu.SemaphoreType.DMA((3,))],
        compiler_params=pltpu.CompilerParams(vmem_limit_bytes=4 << 20),
        cost_estimate=pl.CostEstimate(flops=0, bytes_accessed=1 << 20, transcendentals=0),
        name="outs",
    )(*firsts, *firsts_away, small[0][0], small[1][0], small[0][2], small[1][2], away)
    return (out_volume, out_tiles, out_first, out_second, out_third)


def solution(mesh):
    return jax.shard_map(
        local,
        mesh=mesh,
        in_specs=(
            P("front", "col"),
            P(("front", "col"), None),
            P("front", None),
            P("front", None),
            P("front", "col"),
            P("front", "col"),
            P("front", "col"),
            P("front", None),
            P("front", None),
            P("front", None),
            P(None, "front"),
            P(None, "front"),
            P(),
            P(),
            P("front", None, None),
            P(),
        ),
        out_specs=(P("front", "col"),) * 5,
        check_vma=False,
    )
```

```python
import functools

import jax
import jax.numpy as jnp
from jax import lax
from jax.experimental import pallas as pl
from jax.experimental.pallas import tpu as pltpu
from jax.sharding import PartitionSpec as P

F32 = jnp.float32
BF16 = jnp.bfloat16


def flip(x, mask):
    count = lax.axis_size("front")
    return lax.ppermute(x, "front", [(i, i ^ mask) for i in range(count)])


def shift(x, axis, steps):
    count = lax.axis_size(axis)
    return lax.ppermute(x, axis, [(i, (i + steps) % count) for i in range(count)])


def swap_next(x):
    count = lax.axis_size("front")
    pairs = [(i, i + 2 if i >> 1 & 1 else i - 2) for i in range(count)]
    return lax.ppermute(x, "front", [(i, j) for i, j in pairs if 0 <= j < count])


def mm(a, b):
    return jnp.dot(a, b, preferred_element_type=F32)


def mm_t(a, b):
    return lax.dot_general(a, b, (((0,), (0,)), ((), ())), preferred_element_type=F32)


class Held:
    def __init__(self, source, target, sem):
        self.copy = pltpu.make_async_copy(source, target, sem)
        self.target = target
        self.shape = target.shape
        self.copy.start()

    def wait(self):
        self.copy.wait()

    def __getitem__(self, index):
        return self.target[index]


def kernel(body, outs, args, flops=1e9, fetched=(), scalars=(), scratch=()):
    vmem = pl.BlockSpec(memory_space=pltpu.VMEM)
    specs = [pl.BlockSpec(memory_space=pltpu.HBM) if i in fetched else vmem for i in range(len(args))]
    nbytes = sum(a.size * a.dtype.itemsize for a in args)
    order = sorted(fetched)
    shapes = [cut_shape(fetched, i, args[i]) for i in order]

    def run(*refs):
        ins, rest = list(refs[: len(args)]), refs[len(args) :]
        numbers, rest = rest[: len(scalars)], rest[len(scalars) :]
        results, rest = rest[: len(outs)], rest[len(outs) :]
        own, rest = rest[: len(scratch)], rest[len(scratch) :]
        for k, i in enumerate(order):
            source = ins[i]
            if isinstance(fetched, dict) and fetched[i]:
                source = source.at[fetched[i]]
            ins[i] = Held(source, rest[k], rest[len(order)].at[k])
        body(*ins, *numbers, *results, *own)

    extra = [pltpu.VMEM(shape, args[i].dtype) for i, shape in zip(order, shapes)]
    if order:
        extra.append(pltpu.SemaphoreType.DMA((len(order),)))
    args = [pltpu.with_memory_space_constraint(a, pltpu.HBM) if i in fetched else a for i, a in enumerate(args)]
    return pl.pallas_call(
        run,
        out_shape=[jax.ShapeDtypeStruct(s, t) for s, t in outs],
        in_specs=specs + [pl.BlockSpec(memory_space=pltpu.SMEM)] * len(scalars),
        out_specs=[vmem] * len(outs),
        scratch_shapes=list(scratch) + extra,
        compiler_params=pltpu.CompilerParams(vmem_limit_bytes=10 << 20),
        cost_estimate=pl.CostEstimate(flops=int(flops), bytes_accessed=nbytes, transcendentals=0),
    )(*args, *scalars)


def cut_shape(fetched, i, array):
    cut = fetched[i] if isinstance(fetched, dict) else None
    if not cut:
        return array.shape
    return tuple(len(range(*c.indices(n))) for c, n in zip(cut, array.shape, strict=True))


def block(i, size):
    return pl.ds(pl.multiple_of(i * size, size), size)


def each(count, size, step):
    lax.fori_loop(0, count // size, lambda i, carry: (step(block(i, size)), carry)[1], 0)


def selector_t(row_map):
    order = row_map.shape[1]
    return (row_map == lax.broadcasted_iota(jnp.int32, (order, order), 0)).astype(BF16)


def pack_body(rm1, rm2, d_own, e_own, inv1, inv2, inv3, load2, load3, aimed, out_x, out_c, out_aim):
    front = lax.axis_index("front")
    n2, n3 = inv2.shape[0], inv3.shape[0]
    for x in (rm1, rm2, d_own, e_own, inv1, inv2, inv3, load2, load3):
        x.wait()
    select = selector_t(rm2[pl.ds(front >> 2, 1), :])
    e_t = mm_t(e_own[...], select).astype(BF16)
    out_x[:n2, :] = inv2[...]
    out_x[n2 : 2 * n2, :] = e_t
    out_x[2 * n2 : 2 * n2 + n3, :] = inv3[...]
    out_x[2 * n2 + n3 :, :] = load3[...]
    select = selector_t(rm1[pl.ds(front >> 1, 1), :])
    n1 = inv1.shape[0]
    out_c[:n1, :] = mm_t(d_own[...], select).astype(BF16)
    out_c[n1 : 2 * n1, :] = inv1[...]
    out_c[2 * n1 :, :] = load2[...]
    row = lax.broadcasted_iota(jnp.int32, out_aim.shape, 0)
    out_aim[...] = jnp.where(row == 0, aimed[front, 0] - front, aimed[front, 1] - front)


def leaf_weight_body(rm, c, out_c, out_ct):
    rm.wait()
    c.wait()
    select = selector_t(rm[...])
    size = 256

    def step(i, carry):
        cols = block(i, size)
        own = c[:, cols]
        out_c[:, cols] = mm_t(select, own).astype(BF16)
        out_ct[cols, :] = mm_t(own, select).astype(BF16)
        return carry

    lax.fori_loop(0, c.shape[1] // size, step, 0)


def leaf_term(pieces, columns, c, size):
    col = lax.axis_index("col")
    total = 0.0
    for piece, place in pieces:
        cols = pl.ds(pl.multiple_of(((2 * col + place) & 7) * size, size), piece.shape[0])
        total = total + mm(c[:, cols], mm(piece[...], columns).astype(BF16))
    return total


def near_body(own, up_top, down_low, b, c, load1, out_other, out_mine):
    core = lax.axis_index("front") & 1
    half, size = b.shape[1] // 2, up_top.shape[0]
    for out, which in ((out_other, 1 - core), (out_mine, core)):
        out[...] = -leaf_term(((own, 0), (up_top, 6), (down_low, 3)), b[:, block(which, half)], c, size)
        rows = block(core, load1.shape[0])
        out[rows, :] += load1[:, block(which, half)].astype(F32)


def far_term(up_low, down_top, far_top, far_low, b, c, near, which):
    half, size = b.shape[1] // 2, far_top.shape[0]
    pieces = ((up_low, 7), (down_top, 2), (far_top, 4), (far_low, 5))
    return near[...] - leaf_term(pieces, b[:, block(which, half)], c, size)


def other_body(up_low, down_top, far_top, far_low, b, c, near, out):
    core = lax.axis_index("front") & 1
    out[...] = far_term(up_low, down_top, far_top, far_low, b, c, near, 1 - core).astype(BF16)


def mine_body(up_low, down_top, far_top, far_low, b, c, near, out):
    core = lax.axis_index("front") & 1
    out[...] = far_term(up_low, down_top, far_top, far_low, b, c, near, core)


def first_weight_body(pack, away, load_half, out_d, out_dt, out_inv, out_load):
    front = lax.axis_index("front")
    core = front & 1
    n1 = out_inv.shape[0] // 2
    n2 = away.shape[0] - 2 * n1
    half = out_load.shape[1]
    out_load[...] = jnp.zeros_like(out_load)
    for piece, place in ((pack, core), (away, 1 - core)):
        rows = block(place, n1)
        t = piece[:n1, :]
        out_dt[rows, :] = t
        out_d[:, rows] = t.T
        out_inv[rows, :] = piece[n1 : 2 * n1, :]
        where = block(2 * ((front >> 1) & 1) + place, n2)
        out_load[where, :] = piece[2 * n1 :, block(core, half)]


def second_weight_body(p0, p1, p2, p3, out_e, out_et, out_inv, out_load, out_third):
    front = lax.axis_index("front")
    core = front & 1
    n2 = out_inv.shape[0] // 4
    n3 = n2 // 2
    half = out_load.shape[1]
    out_load[...] = jnp.zeros_like(out_load)
    for mask, piece in enumerate((p0, p1, p2, p3)):
        place = (front & 3) ^ mask
        rows = block(place, n2)
        t = piece[n2 : 2 * n2, :]
        out_inv[rows, :] = piece[:n2, :]
        out_et[rows, :] = t
        out_e[:, rows] = t.T
        out_third[block(place, n3), :] = piece[2 * n2 : 2 * n2 + n3, :]
        out_load[block(((front >> 2) & 1) * 4 + place, n3), :] = piece[2 * n2 + n3 :, block(core, half)]


def first_body(mine, other, inv, d, load2, out_rhs, *terms):
    rhs = (mine[...] + other[...].astype(F32)).astype(BF16)
    out_rhs[...] = rhs
    y = mm(inv[...], rhs).astype(BF16)
    term = (load2[...].astype(F32) - mm(d[...], y)).astype(BF16)
    size = term.shape[1] // len(terms)
    for i, out in enumerate(terms):
        out[...] = term[:, i * size : (i + 1) * size]


def second_body(part, mine, other, inv, e, load3, out_rhs, out_term):
    size = mine.shape[1]
    rhs = (mine[...].astype(F32) + other[...].astype(F32)).astype(BF16)
    out_rhs[...] = rhs
    y = mm(inv[...], rhs).astype(BF16)
    out_term[...] = (load3[:, part * size : (part + 1) * size].astype(F32) - mm(e[...], y)).astype(BF16)


def down_body(part, mine, other, third_near, third_far, e_t, inv2, rhs2, d_t, inv1, rhs1, out1, own2, away2, own3, away3, out3, out2):
    front = lax.axis_index("front")
    bit = (front >> 2) & 1
    size = mine.shape[1]
    rhs = (mine[...].astype(F32) + other[...].astype(F32)).astype(BF16)
    rows = third_near.shape[0]
    out3[block(bit, rows), :] = mm(third_near[...], rhs).astype(BF16)
    out3[block(1 - bit, rows), :] = mm(third_far[...], rhs).astype(BF16)
    left = (rhs2[...].astype(F32) - mm(e_t[...], out3[...])).astype(BF16)
    sol = mm(inv2[...], left).astype(BF16)
    out2[...] = sol
    left = (rhs1[:, part * size : (part + 1) * size].astype(F32) - mm(d_t[...], sol)).astype(BF16)
    out1[...] = mm(inv1[...], left).astype(BF16)
    for own, away, whole, place in ((own2, away2, out2, front & 3), (own3, away3, out3, front & 7)):
        own[...] = whole[block(place, own.shape[0]), :]
        away[...] = whole[block(place ^ 1, own.shape[0]), :]


def merge_body(second_a, second_b, third_a, third_b, out):
    rows, size = second_a.shape
    out[:rows, :size] = second_a[...]
    out[:rows, size:] = second_b[...]
    out[rows:, :size] = third_a[...]
    out[rows:, size:] = third_b[...]


def copy_all(pairs, sems):
    copies = [pltpu.make_async_copy(x, y, sems.at[i]) for i, (x, y) in enumerate(pairs)]
    for copy in copies:
        copy.start()
    for copy in copies:
        copy.wait()


def stage_body(b, surface, out_b, out_surface, sems):
    copy_all([(b, out_b), (surface, out_surface)], sems)


def factor_body(own, up_top, up_low, down_top, down_low, far_top, far_low, out, sems):
    col = lax.axis_index("col")
    size = up_top.shape[0]
    pairs = []
    for piece, place in ((own, 0), (up_top, 6), (up_low, 7), (down_top, 2), (down_low, 3), (far_top, 4), (far_low, 5)):
        rows = pl.ds(pl.multiple_of(((2 * col + place) & 7) * size, size), piece.shape[0])
        pairs.append((piece, out.at[rows, :]))
    copy_all(pairs, sems)


def chunk_of(core, part, size):
    return slice((2 * core + part) * size, (2 * core + part + 1) * size)


def store_chunks(source, out, part, size, sems):
    stores = []
    for i in (0, 1):
        stores.append(
            pltpu.make_async_copy(source.at[:, i * size : (i + 1) * size], out.at[:, chunk_of(i, part, size)], sems.at[i])
        )
        stores[-1].start()
    return stores


def volume_body(part, c_t, b, factor, surface, s_own, s_away, aim, *rest):
    out, out_v, out_near, out_relay, out_up, out_down, left, sems = rest[-8:]
    core = lax.axis_index("front") & 1
    size = s_own.shape[1]
    sides = (jnp.where(core == 0, s_own[...], s_away[...]), jnp.where(core == 0, s_away[...], s_own[...]))
    side = jnp.concatenate(sides, axis=1)

    def start(rows):
        load = jnp.concatenate([b[rows, chunk_of(i, part, size)] for i in (0, 1)], axis=1)
        left[rows, :] = (load.astype(F32) - mm(c_t[rows, :], side)).astype(BF16)

    def solve(rows):
        out_v[rows, :] = mm(factor[rows, :], left[...]).astype(BF16)

    each(b.shape[0], 256, start)
    each(b.shape[0], 256, solve)
    stores = store_chunks(out_v, out, part, size, sems)
    inner = 1 - 2 * core

    def tiles(rows):
        v = out_v[...]
        c_one = mm(surface[1, rows, :], v).astype(BF16)
        c_two = mm(surface[2, rows, :], v).astype(BF16)
        zero = jnp.zeros_like(c_one)
        one = jnp.broadcast_to(aim[0:1, 0:1], c_one.shape)
        two = jnp.broadcast_to(aim[1:2, 0:1], c_one.shape)
        for out, offset in ((out_near, inner), (out_relay, -inner), (out_up, 2), (out_down, -2)):
            out[rows, :] = jnp.where(one == offset, c_one, jnp.where(two == offset, c_two, zero))

    each(surface.shape[1], 256, tiles)
    for store in stores:
        store.wait()


def sum_body(up, down, relay, out_inner, out_outer):
    front = lax.axis_index("front")
    core = front & 1
    even = (front >> 1) & 1 == 0
    for which in (0, 1):
        for parity in (True, False):

            @pl.when((core == which) & (even == parity))
            def _():
                to_up, to_down = (out_inner, out_outer) if parity else (out_outer, out_inner)
                to_up[...] = up[...] + relay[...] if which == 0 else up[...]
                to_down[...] = down[...] + relay[...] if which == 1 else down[...]


def outs_body(first_a, first_b, first_away_a, first_away_b, second_a, second_b, third_a, third_b, away, out1, out2, out3, t1, t2, t3, sems):
    core = lax.axis_index("front") & 1
    size = first_a.shape[1]
    rows = block(core, t1.shape[0])
    n2 = t2.shape[0]
    copies = []
    for i, (out, total, own, theirs) in enumerate((
        (out1, t1, (first_a.at[rows, :], first_b.at[rows, :]), (first_away_a.at[rows, :], first_away_b.at[rows, :])),
        (out2, t2, (second_a, second_b), (away.at[:n2, :size], away.at[:n2, size:])),
        (out3, t3, (third_a, third_b), (away.at[n2:, :size], away.at[n2:, size:])),
    )):
        for part in (0, 1):
            total[:, block(2 * core + part, size)] = own[part][...]
            total[:, block(2 * (1 - core) + part, size)] = theirs[part][...]
        copies.append(pltpu.make_async_copy(total, out, sems.at[i]))
        copies[-1].start()
    for copy in copies:
        copy.wait()


def own_body(surface, v, out):
    def tiles(rows):
        out[rows, :] = mm(surface[0, rows, :], v[...]).astype(BF16)

    each(surface.shape[1], 256, tiles)


def finish_body(part, own, near, back, ahead, *rest):
    out, total, sems = rest[-3:]
    size, tile = own.shape[1] // 2, own.shape[0] // 4
    stores = []
    for k in range(4):
        rows = slice(k * tile, (k + 1) * tile)
        total[rows, :] = (
            own[rows, :].astype(F32) + near[rows, :].astype(F32) + back[rows, :].astype(F32) + ahead[rows, :].astype(F32)
        ).astype(BF16)
        stores += store_chunks(total.at[rows, :], out.at[rows, :], part, size, sems.at[2 * k : 2 * k + 2])
    for store in stores:
        store.wait()


VMEM = pl.BlockSpec(memory_space=pltpu.VMEM)
SMEM = pl.BlockSpec(memory_space=pltpu.SMEM)
HBM = pl.BlockSpec(memory_space=pltpu.HBM)


def halves(body, args, scalars, extra_outs, scratch, whole, flops):
    shape = jax.ShapeDtypeStruct((args[0].shape[0], 2 * extra_outs[0].shape[1]), BF16) if whole is None else whole
    more = () if whole is None else (whole,)
    return pl.pallas_call(
        body,
        out_shape=[jax.ShapeDtypeStruct(shape.shape, BF16)] + extra_outs[1:],
        in_specs=[VMEM] * len(args) + [SMEM] * len(scalars) + [HBM] * len(more),
        out_specs=[HBM] + [VMEM] * len(extra_outs[1:]),
        scratch_shapes=scratch + [pltpu.SemaphoreType.DMA((8,))],
        input_output_aliases={len(args) + len(scalars): 0} if more else {},
        compiler_params=pltpu.CompilerParams(vmem_limit_bytes=12 << 20),
        cost_estimate=pl.CostEstimate(flops=int(flops), bytes_accessed=8 << 20, transcendentals=0),
    )(*args, *scalars, *more)


def stage(body, shapes, args):
    args = [pltpu.with_memory_space_constraint(a, pltpu.HBM) for a in args]
    return pl.pallas_call(
        body,
        out_shape=[jax.ShapeDtypeStruct(x, BF16) for x in shapes],
        in_specs=[HBM] * len(args),
        out_specs=[VMEM] * len(shapes),
        scratch_shapes=[pltpu.SemaphoreType.DMA((len(args),))],
        compiler_params=pltpu.CompilerParams(vmem_limit_bytes=2 << 20),
        cost_estimate=pl.CostEstimate(flops=0, bytes_accessed=8 << 20, transcendentals=0),
    )(*args)


def local(
    leaf_load,
    leaf_inverse,
    leaf_coupling,
    leaf_rowmap,
    load_first,
    load_second,
    load_third,
    inverse_first,
    inverse_second,
    inverse_third,
    coupling_first,
    coupling_second,
    rowmap_first,
    rowmap_second,
    surface_coupling,
    neighbor_tiles,
):
    full, panel = leaf_load.shape
    half = panel // 2
    order = leaf_coupling.shape[0]
    square = ((order, order), BF16)
    column = ((order, half), BF16)

    rows = leaf_inverse.shape[0]
    top, low = leaf_inverse[: rows // 2], leaf_inverse[rows // 2 :]
    up_top = shift(top, "col", 1)
    down_low = shift(low, "col", -1)
    up_low = shift(low, "col", 1)
    down_top = shift(top, "col", -1)
    far_top = shift(up_top, "col", 1)
    far_low = shift(down_low, "col", -1)

    n1, n2, n3 = inverse_first.shape[0], inverse_second.shape[0], inverse_third.shape[0]
    pack_x, pack_c, aim = kernel(
        pack_body,
        [((2 * n2 + 2 * n3, order), BF16), ((2 * n1 + n2, order), BF16), ((8, 128), jnp.int32)],
        (rowmap_first, rowmap_second, coupling_first, coupling_second, inverse_first, inverse_second, inverse_third, load_second, load_third),
        fetched=range(9),
        scalars=(neighbor_tiles,),
    )
    pack2 = flip(pack_x, 2)
    pack1 = flip(pack_x, 1)
    away_c = flip(pack_c, 1)
    leaf_c, leaf_ct = kernel(
        leaf_weight_body, [((order, full), BF16), ((full, order), BF16)], (leaf_rowmap, leaf_coupling), fetched=range(2)
    )
    first_d, first_dt, first_inv, load2 = kernel(
        first_weight_body, [square, square, square, column], (pack_c, away_c, load_second)
    )
    pack3 = flip(pack2, 1)
    second_e, second_et, second_inv, load3, third_near = kernel(
        second_weight_body, [square, square, square, column, ((order // 2, order), BF16)], (pack_x, pack1, pack2, pack3)
    )
    third_far = flip(third_near, 6)

    near_other, near_mine = kernel(
        near_body, [((order, half), F32)] * 2, (leaf_inverse, up_top, down_low, leaf_load, leaf_c, load_first), 2e9
    )
    (other,) = kernel(other_body, [column], (up_low, down_top, far_top, far_low, leaf_load, leaf_c, near_other))
    other = flip(other, 1)
    (mine,) = kernel(mine_body, [((order, half), F32)], (up_low, down_top, far_top, far_low, leaf_load, leaf_c, near_mine))
    piece = ((order, half // 2), BF16)
    rhs_first, *terms = kernel(first_body, [column, piece, piece], (mine, other, first_inv, first_d, load2))
    aways = []
    for part in range(2):
        aways.append(flip(terms[part], 2))
    load, surface = stage(stage_body, [leaf_load.shape, surface_coupling.shape], (leaf_load, surface_coupling))
    (factor,) = stage(factor_body, [(full, full)], (leaf_inverse, up_top, up_low, down_top, down_low, far_top, far_low))
    rhs_second, aways_second, terms_second = [], [], []
    for part in range(2):
        rhs, term = kernel(
            functools.partial(second_body, part),
            [piece, piece],
            (terms[part], aways[part], second_inv, second_e, load3),
        )
        aways_second.append(flip(term, 6))
        rhs_second.append(rhs)
        terms_second.append(term)
    firsts, firsts_away, small = [], [], []
    for part in range(2):
        first, *rest = kernel(
            functools.partial(down_body, part),
            [piece] + [((n, half // 2), BF16) for n in (n2, n2, n3, n3)],
            (terms_second[part], aways_second[part], third_near, third_far, second_et, second_inv, rhs_second[part], first_dt, first_inv, rhs_first),
            scratch=[pltpu.VMEM(*piece)] * 2,
        )
        firsts_away.append(flip(first, 1))
        firsts.append(first)
        small.append(rest)

    tail = []
    out_volume = out_tiles = None
    part_shape = jax.ShapeDtypeStruct((full, half), BF16)
    part_scratch = pltpu.VMEM((full, half), BF16)
    for part in range(2):
        out_volume, volume, near, relay, ahead_sum, back_sum = halves(
            functools.partial(volume_body, part),
            (leaf_ct, load, factor, surface, firsts[part], firsts_away[part], aim),
            (),
            [part_shape] * 6,
            [part_scratch],
            out_volume,
            3e9,
        )
        relay = flip(relay, 1)
        inner, outer = kernel(sum_body, [((full, half), BF16)] * 2, (ahead_sum, back_sum, relay), 1e6)
        from_outer = swap_next(outer)
        from_inner = flip(inner, 2)
        near = flip(near, 1)
        (c_own,) = kernel(own_body, [((full, half), BF16)], (surface, volume))
        tail.append((c_own, near, from_outer, from_inner))
    for part, terms in enumerate(tail):
        (out_tiles,) = halves(
            functools.partial(finish_body, part), terms, (), [part_shape], [part_scratch], out_tiles, 1e6
        )

    (away,) = kernel(merge_body, [((n2 + n3, half), BF16)], (small[0][1], small[1][1], small[0][3], small[1][3]), 1e6)
    away = flip(away, 1)
    shapes = [(n1, panel), (n2, panel), (n3, panel)]
    out_first, out_second, out_third = pl.pallas_call(
        outs_body,
        out_shape=[jax.ShapeDtypeStruct(x, BF16) for x in shapes],
        in_specs=[VMEM] * 9,
        out_specs=[HBM] * 3,
        scratch_shapes=[pltpu.VMEM(x, BF16) for x in shapes] + [pltpu.SemaphoreType.DMA((3,))],
        compiler_params=pltpu.CompilerParams(vmem_limit_bytes=4 << 20),
        cost_estimate=pl.CostEstimate(flops=0, bytes_accessed=1 << 20, transcendentals=0),
        name="outs",
    )(*firsts, *firsts_away, small[0][0], small[1][0], small[0][2], small[1][2], away)
    return (out_volume, out_tiles, out_first, out_second, out_third)


def solution(mesh):
    return jax.shard_map(
        local,
        mesh=mesh,
        in_specs=(
            P("front", "col"),
            P(("front", "col"), None),
            P("front", None),
            P("front", None),
            P("front", "col"),
            P("front", "col"),
            P("front", "col"),
            P("front", None),
            P("front", None),
            P("front", None),
            P(None, "front"),
            P(None, "front"),
            P(),
            P(),
            P("front", None, None),
            P(),
        ),
        out_specs=(P("front", "col"),) * 5,
        check_vma=False,
    )
```
